256 devices in a mesh: section: 4 (over x), expert: 32 (over z, y), mp: 2 (over core).
Axes of the slice: x: 4, y: 4, z: 8, core: 2. Of those that a mesh axis runs over, the one named last changes fastest.
Arguments:
- out_grad: bfloat16 [4, 4096, 4096], P('section', 'expert', 'mp'), may hold values from -6 to 6
- expert_ids: int32 [4, 4096, 2], P('section', 'expert'), may hold values from 0 to 31, all different within a row; in each aligned block of 128 rows (0 to 127, 128 to 255, ..., all dimensions but the last counted through in order) at most 16 rows name the same one
- gate_codes: int32 [4, 4096, 2], P('section', 'expert'), may hold values from 1 to 255
- up_weight: bfloat16 [4, 32, 4096, 1024], P('section', 'expert', None, 'mp'), may hold values from -0.09375 to 0.09375
- down_weight: bfloat16 [4, 32, 1024, 4096], P('section', 'expert', 'mp'), may hold values from -0.1875 to 0.1875
- pre_act: bfloat16 [4, 32, 512, 1024], P('section', 'expert', None, 'mp'), may hold values from -6 to 6
- conv_grad: bfloat16 [4, 4096, 4096], P('section', 'expert', 'mp'), may hold values from -6 to 6
- conv_input: bfloat16 [4, 4096, 4096], P('section', 'expert', 'mp'), may hold values from -0.09375 to 0.09375
- conv_weight: float32 [4, 4, 4096], P('section', None, 'mp'), may hold values from -3 to 3
- in_proj: bfloat16 [4, 4096, 4096], P('section', 'expert', 'mp'), may hold values from -0.09375 to 0.09375
Outputs:
- residual_to_previous: bfloat16 [4, 4096, 4096], P('section', 'expert', 'mp')
- kernel_grad: float32 [4, 4, 4096], P('section', None, 'mp')
The draws below stay inside these ranges and needn't reach their ends.
Inputs may be any that keep to these rules, and one draw needn't show every extreme that they name: `expert_ids`: each token names two different experts; in every section, the tokens of one block of 128 name no expert more than 16 times, a bound that some block reaches.
All inputs are finite; a program needn't handle non-finite values.
Results may differ from the reference program's by a relative error of at most 0.0044.
Values may be sent and summed in bfloat16 or wider, within the bound.
A program may use at most 128 MiB of HBM per device.

```python
import math
import jax
import jax.numpy as jnp
import numpy as np
from jax import lax

D = 4096
FF = 1024
CH = 4096
KERNEL = 4
TOK_DEV = 128
TOKENS = 4096
EXPERTS = 32
CAP = 16
SLOTS = 512
N_SECTION = 4
N_EXPERT = 32


def place_ends(array, rng, least, high):
    shape = array.shape
    spot = [jax.random.randint(jax.random.fold_in(rng, axis), (), 0, shape[axis]) for axis in range(len(shape))]
    array = array.at[tuple(spot)].set(least)
    longest = shape.index(max(shape))
    spot[longest] = (spot[longest] + 1) % shape[longest]
    return array.at[tuple(spot)].set(high)


def steps_of(key, dims, cuts, smallest, high):
    level, own = 1.0, jax.random.fold_in(key, 6)
    for position, shards_of in cuts:
        draws = jnp.exp(jax.random.uniform(jax.random.fold_in(own, position), (shards_of,), jnp.float32, smallest / len(cuts), high / len(cuts)))
        level = level * jnp.repeat(draws, dims[position] // shards_of).reshape([-1 if axis == position else 1 for axis in range(len(dims))])
    return level


def shared_out(own_key, own, number, rows, amount, top, reach, slope):
    order = jax.random.permutation(own_key, amount)
    crowded, common = shares(amount, rows * top, reach, slope, True), shares(amount, rows * top, reach, slope, False)
    places = jnp.arange(amount)

    def named(tallies, offset_by):
        used = int((tallies > 0).sum())
        fixed = max(1, used // 4)
        passed = fixed + (places - fixed + offset_by * (used - fixed)) % max(1, amount - fixed)
        return jnp.zeros((amount,), jnp.int32).at[order[jnp.where(places < fixed, places, passed)]].set(jnp.asarray(tallies, jnp.int32))

    tallies = jnp.where(number % 4 == 0, named(crowded, number // 4), named(common, number - number // 4 - 1))
    mixed = jax.random.permutation(jax.random.fold_in(own, 3), amount)
    source_of, receiver = mixed[0:amount // 2 * 2:2], mixed[1:amount // 2 * 2:2]
    room = jnp.minimum(tallies[source_of] - 1, reach - tallies[receiver]) // 2
    room = jnp.where((source_of == order[0]) | (receiver == order[0]) | (tallies[receiver] == 0), 0, jnp.maximum(room, 0))
    passed = jax.random.randint(jax.random.fold_in(own, 4), (amount // 2,), 0, 1 << 20) % (room + 1)
    tallies = tallies.at[source_of].add(-passed).at[receiver].add(passed)
    labels = jnp.searchsorted(jnp.cumsum(tallies), jnp.arange(rows * top), side="right").astype(jnp.int32)
    table = labels.reshape(top, rows).T
    table = table[jax.random.permutation(jax.random.fold_in(own, 1), rows)]
    offset_by = jax.random.randint(jax.random.fold_in(own, 2), (rows, 1), 0, top)
    return jnp.take_along_axis(table, (jnp.arange(top)[None, :] + offset_by) % top, axis=1)


def shares(amount, total, limit, skew, full):
    weights = [(1 << 20) // math.isqrt(grade ** skew) + 1 for grade in range(1, amount + 1)]
    largest = limit if full else min(limit, max(-(-total // amount), total * weights[0] // sum(weights)))
    least = 1 if total - largest >= amount - 1 else 0
    holding, surplus = [largest] + [least] * (amount - 1), total - largest - least * (amount - 1)
    while surplus > 0:
        free = [i for i in range(1, amount) if holding[i] < largest] or [i for i in range(1, amount) if holding[i] < limit]
        pool, left = sum([weights[i] for i in free]), surplus
        for i in free:
            addition = min(limit - holding[i], max(1, left * weights[i] // pool), surplus)
            holding[i] = holding[i] + addition
            surplus = surplus - addition
    return np.array(holding)


def normal_values(key, shape, deviation, reach, cuts=(), held_as=jnp.bfloat16):
    array = deviation * jax.random.normal(key, shape, jnp.float32)
    if cuts:
        array = array * steps_of(key, shape, cuts, -0.22, 0.18)
    return jnp.clip(array, -reach, reach).astype(held_as)


def setup_inputs(seed: int = 0) -> dict:
    arg_keys = jax.random.split(jax.random.key(seed), 11)
    out_grad = normal_values(arg_keys[0], (N_SECTION, TOKENS, D), 1.0, 6.0, ((0, 4), (1, 32), (2, 2)))
    expert_ids_keys = jax.random.split(jax.random.fold_in(arg_keys[1], 1), N_SECTION * TOKENS // TOK_DEV)
    expert_ids_turns = jax.random.permutation(jax.random.fold_in(arg_keys[1], 3), N_SECTION * TOKENS // TOK_DEV)
    expert_ids = jax.vmap(lambda own, number: shared_out(jax.random.fold_in(arg_keys[1], 2), own, number, TOK_DEV, EXPERTS, 2, CAP, 2))(expert_ids_keys, expert_ids_turns).reshape((N_SECTION, TOKENS, 2))
    gate_codes = place_ends(jax.random.randint(arg_keys[2], (N_SECTION, TOKENS, 2), 1, 256), jax.random.fold_in(arg_keys[2], 1), 1, 255).astype(jnp.int32)
    up_weight = normal_values(arg_keys[3], (N_SECTION, EXPERTS, D, FF), D ** -0.5, 0.09375, ((0, 4), (1, 32), (3, 2)))
    down_weight = normal_values(arg_keys[4], (N_SECTION, EXPERTS, FF, D), FF ** -0.5, 0.1875, ((0, 4), (1, 32), (2, 2)))
    pre_act = normal_values(arg_keys[5], (N_SECTION, EXPERTS, SLOTS, FF), 1.0, 6.0, ((0, 4), (1, 32), (3, 2)))
    conv_grad = normal_values(arg_keys[6], (N_SECTION, TOKENS, CH), 1.0, 6.0, ((0, 4), (1, 32), (2, 2)))
    conv_input = normal_values(arg_keys[7], (N_SECTION, TOKENS, CH), (1.0 / TOKENS ** 0.5), 0.09375, ((0, 4), (1, 32), (2, 2)))
    conv_weight = normal_values(arg_keys[8], (N_SECTION, KERNEL, CH), 0.5, 3.0, ((0, 4), (2, 2)), jnp.float32)
    in_proj = normal_values(arg_keys[9], (N_SECTION, D, CH), CH ** -0.5, 0.09375, ((0, 4), (1, 32), (2, 2)))
    return {"out_grad": out_grad, "expert_ids": expert_ids, "gate_codes": gate_codes, "up_weight": up_weight, "down_weight": down_weight, "pre_act": pre_act, "conv_grad": conv_grad, "conv_input": conv_input, "conv_weight": conv_weight, "in_proj": in_proj}


def silu_slope(pre_value):
    sig = jax.nn.sigmoid(pre_value)
    return sig * (1.0 + pre_value * (1.0 - sig))


def slot_targets(route_ids):
    blocks = route_ids.reshape(N_EXPERT, TOK_DEV * 2)
    onehot = (blocks[:, :, None] == jnp.arange(EXPERTS, dtype=jnp.int32)[None, None, :]).astype(jnp.int32)
    before = jnp.cumsum(onehot, axis=1) - onehot
    rank = jnp.sum(before * onehot, axis=2)
    source = jnp.arange(N_EXPERT, dtype=jnp.int32)[:, None]
    return (source * CAP + rank).reshape(TOKENS * 2).astype(jnp.int32)


def section_moe(grad_rows, route_ids, codes, up_section, down_section, pre_section):
    gates = codes.astype(jnp.float32) / 256.0
    slots = slot_targets(route_ids)
    owners = route_ids.reshape(TOKENS * 2).astype(jnp.int32)
    scaled = (gates[:, :, None] * grad_rows.astype(jnp.float32)[:, None, :]).astype(jnp.bfloat16)
    scaled = scaled.reshape(TOKENS * 2, D)

    def one_expert(items):
        number, up_one, down_one, pre_one = items
        places = jnp.where(owners == number, slots, SLOTS)
        rows = jnp.zeros((SLOTS, D), jnp.bfloat16).at[places].set(scaled, mode="drop")
        hidden = jnp.dot(rows, down_one.T, preferred_element_type=jnp.float32)
        pre_grad = (hidden * silu_slope(pre_one.astype(jnp.float32))).astype(jnp.bfloat16)
        return jnp.dot(pre_grad, up_one.T, preferred_element_type=jnp.float32).astype(jnp.bfloat16)

    slot_grad = lax.map(one_expert, (jnp.arange(EXPERTS, dtype=jnp.int32), up_section, down_section, pre_section))
    picked = slot_grad[owners, slots].astype(jnp.float32).reshape(TOKENS, 2, D)
    return grad_rows.astype(jnp.float32) + picked[:, 0, :] + picked[:, 1, :]


def section_conv(grad_conv, input_conv, taps):
    grad_full = grad_conv.astype(jnp.float32)
    input_full = input_conv.astype(jnp.float32)
    padded_grad = jnp.pad(grad_full, ((0, KERNEL - 1), (0, 0)))
    result = jnp.zeros((TOKENS, CH), jnp.float32)
    for tap in range(KERNEL):
        start = KERNEL - 1 - tap
        result = result + taps[tap][None, :] * padded_grad[start:start + TOKENS]
    padded_input = jnp.pad(input_full, ((KERNEL - 1, 0), (0, 0)))
    tap_grads = jnp.stack([jnp.sum(grad_full * padded_input[tap:tap + TOKENS], axis=0) for tap in range(KERNEL)])
    return result.astype(jnp.bfloat16), tap_grads


def reference(out_grad, expert_ids, gate_codes, up_weight, down_weight, pre_act, conv_grad, conv_input, conv_weight, in_proj):
    residuals = []
    kernels = []
    for section_index in range(N_SECTION):
        moe_total = section_moe(out_grad[section_index], expert_ids[section_index], gate_codes[section_index], up_weight[section_index], down_weight[section_index], pre_act[section_index])
        input_grad, tap_grads = section_conv(conv_grad[section_index], conv_input[section_index], conv_weight[section_index])
        proj_grad = jnp.dot(input_grad, in_proj[section_index].T, preferred_element_type=jnp.float32)
        residuals.append((moe_total + proj_grad).astype(jnp.bfloat16))
        kernels.append(tap_grads)
    residuals = residuals[1:] + [jnp.zeros((TOKENS, D), jnp.bfloat16)]
    return jnp.stack(residuals), jnp.stack(kernels)
```

```python
import jax
import jax.numpy as jnp
from jax import lax
from jax.experimental import pallas as pl
from jax.experimental.pallas import tpu as pltpu
from jax.sharding import PartitionSpec as P

MESH = pl.DeviceIdType.MESH
F32 = jnp.float32
BF16 = jnp.bfloat16

NY = 4
NZ = 8
CAP = 16
TOK = 128
HALF = 2048
NSEC = 4
NEXP = 32
NT = (((1,), (1,)), ((), ()))


def dot_nt(a, b):
    return lax.dot_general(a, b, NT, preferred_element_type=F32)


def silu_slope(pre_value):
    sig = 1.0 / (1.0 + jnp.exp(-pre_value))
    return sig * (1.0 + pre_value * (1.0 - sig))


def kernel(
    og, ids, codes, cg, ci, cw, bp, up, down, pre,
    out, kout,
    wdn, wup, prev_, sbuf, xin, yout, ret, comb, comb_r, og_r,
    bg, ag, halo_g, halo_i, gext, iext, part, part_r, psend, prec,
    tap_p, tap_r, tap_s, tap_z, tap_t, tap_o,
    lsem, wsend, wrecv, hsend, hrecv, osend, orecv,
    bsend, brecv, xsend, xrecv, ysend, yrecv, asend, arecv,
    psem_s, psem_r, qsend, qrecv, tsend, trecv,
):
    sec = lax.axis_index("section")
    me = lax.axis_index("expert")
    core = lax.axis_index("mp")
    z = me // NY
    y = me % NY
    mine = z // 4
    other = 1 - core
    partner = (sec, me, other)

    def rcopy(src, dst, ssem, rsem, dev):
        return pltpu.make_async_remote_copy(
            src_ref=src, dst_ref=dst, send_sem=ssem, recv_sem=rsem,
            device_id=dev, device_id_type=MESH,
        )

    def wait_in(dst, rsem):
        rcopy(dst, dst, lsem.at[0], rsem, partner).wait_recv()

    def wait_out(src, ssem):
        rcopy(src, src, ssem, lsem.at[0], partner).wait_send()

    def zdev(dz):
        return (sec, ((z + dz + NZ) % NZ) * NY + y, core)

    def ydev(dy):
        return (sec, z * NY + (y + dy) % NY, core)

    def rows(start, size):
        return pl.ds(pl.multiple_of(start, size), size)

    has_next = me < NEXP - 1
    has_prev = me > 0
    halo_g_out = rcopy(cg.at[pl.ds(0, 16)], halo_g, hsend.at[0], hrecv.at[0], (sec, me - 1, core))
    halo_i_out = rcopy(ci.at[pl.ds(TOK - 16, 16)], halo_i, hsend.at[1], hrecv.at[1], (sec, me + 1, core))

    @pl.when(has_prev)
    def _():
        halo_g_out.start()

    @pl.when(has_next)
    def _():
        halo_i_out.start()

    def ring(step, up_way):
        shard = (z - (step - 1) + NZ) % NZ if up_way else (z + (step - 1)) % NZ
        way = 0 if up_way else 1
        start, size = (0, TOK) if step < 4 else ((0, 64) if up_way else (64, 64))
        block = pl.ds(pl.multiple_of(shard * TOK + start, 64), size)
        src = bp if step == 1 else bg.at[block]
        return rcopy(src, bg.at[block], bsend.at[step - 1, way], brecv.at[step - 1, way], zdev(1 if up_way else -1))

    def ring_arrived(step):
        for way in range(2):
            shard = (z - step + NZ) % NZ if way == 0 else (z + step) % NZ
            start, size = (0, TOK) if step < 4 else ((0, 64) if way == 0 else (64, 64))
            block = pl.ds(pl.multiple_of(shard * TOK + start, 64), size)
            wait_in(bg.at[block], brecv.at[step - 1, way])

    def ring_go(step):
        if step > 1:
            ring_arrived(step - 1)
        ring(step, True).start()
        ring(step, False).start()

    own_rows = pltpu.make_async_copy(bp, bg.at[rows(z * TOK, TOK)], lsem.at[4])
    own_down = pltpu.make_async_copy(down, wdn.at[core], lsem.at[1])
    own_up = pltpu.make_async_copy(up, wup.at[core], lsem.at[2])
    own_pre = pltpu.make_async_copy(pre.at[rows(core * 256, 256)], prev_.at[core], lsem.at[3])
    give_down = rcopy(down, wdn.at[core], wsend.at[0], wrecv.at[0], partner)
    give_up = rcopy(up, wup.at[core], wsend.at[1], wrecv.at[1], partner)
    give_pre = rcopy(pre.at[rows(other * 256, 256)], prev_.at[core], wsend.at[2], wrecv.at[2], partner)
    give_og = rcopy(og, og_r, osend.at[0], orecv.at[0], (sec - 1, me, core))
    give_comb = rcopy(comb, comb_r, osend.at[1], orecv.at[1], (sec - 1, me, core))

    active = sec > 0

    def block_copy(e):
        return rcopy(
            sbuf.at[rows(e * CAP, CAP)],
            xin.at[core, rows((me % 16) * CAP, CAP)],
            xsend.at[e], xrecv.at[me % 16, core], (sec, e, mine),
        )

    def block_local(e):
        return pltpu.make_async_copy(
            sbuf.at[rows(e * CAP, CAP)],
            xin.at[core, rows((me % 16) * CAP, CAP)],
            xrecv.at[me % 16, core],
        )

    @pl.when(active)
    def _():
        ring_go(1)
        own_rows.start()

        lane = lax.broadcasted_iota(jnp.int32, (TOK, NEXP * CAP), 1)
        expert = lane // CAP
        rank = lane % CAP
        first = ids[:, 0:1] == expert
        second = ids[:, 1:2] == expert
        named = first | second
        gates = codes[...].astype(F32) / 256.0
        gate = jnp.where(first, gates[:, 0:1], 0.0) + jnp.where(second, gates[:, 1:2], 0.0)
        low = lax.broadcasted_iota(jnp.int32, (TOK, TOK), 1) < lax.broadcasted_iota(jnp.int32, (TOK, TOK), 0)
        before = jnp.dot(
            jnp.where(low, 1.0, 0.0).astype(BF16),
            jnp.where(named, 1.0, 0.0).astype(BF16),
            preferred_element_type=F32,
        )
        here = named & (before == rank.astype(F32))
        comb[...] = jnp.where(here, 1.0, 0.0).astype(BF16)
        placed = jnp.where(here, gate, 0.0).T.astype(BF16)
        for tile in range(4):
            cols = pl.ds(tile * 512, 512)
            sbuf[:, cols] = jnp.dot(placed, og[:, cols], preferred_element_type=F32).astype(BF16)

        def send_block(i, carry):
            turn = i // 8
            zt = (z - turn + 8) % 4 + 4 * ((i // 4) % 2)
            e = zt * NY + (y + i) % NY
            own = (e == me) & (mine == core)

            @pl.when(own)
            def _():
                block_local(e).start()

            @pl.when(jnp.logical_not(own))
            def _():
                block_copy(e).start()

            return carry

        lax.fori_loop(0, NEXP, send_block, 0)
        own_down.start()
        own_up.start()
        own_pre.start()
        give_down.start()
        give_pre.start()
        give_up.start()
        give_og.start()
        give_comb.start()

    @pl.when(has_next)
    def _():
        wait_in(halo_g, hrecv.at[0])

    @pl.when(jnp.logical_not(has_next))
    def _():
        halo_g[...] = jnp.zeros_like(halo_g)

    @pl.when(has_prev)
    def _():
        wait_in(halo_i, hrecv.at[1])

    @pl.when(jnp.logical_not(has_prev))
    def _():
        halo_i[...] = jnp.zeros_like(halo_i)

    gext[pl.ds(0, TOK), :] = cg[...].astype(F32)
    gext[pl.ds(TOK, 8), :] = halo_g[...].astype(F32)[0:8]
    iext[pl.ds(0, 8), :] = halo_i[...].astype(F32)[8:16]
    iext[pl.ds(8, TOK), :] = ci[...].astype(F32)
    tap_p[...] = jnp.zeros_like(tap_p)

    for quarter in range(4):
        @pl.loop(0, 4)
        def _(i):
            cols = pl.ds(pl.multiple_of(quarter * 512 + i * 128, 128), 128)
            lanes = pl.ds(pl.multiple_of(i * 128, 128), 128)
            grad = gext[pl.ds(0, TOK), cols]
            total = jnp.zeros((TOK, 128), F32)
            for tap in range(4):
                total = total + cw[tap : tap + 1, cols] * gext[pl.ds(3 - tap, TOK), cols]
                term = grad * iext[pl.ds(5 + tap, TOK), cols]
                tap_p[quarter, tap : tap + 1, lanes] = jnp.sum(term, axis=0, keepdims=True)
            ag[rows(y * TOK, TOK), cols] = total.astype(BF16)

    def tap_scatter(dy):
        to = (y + dy) % NY
        return rcopy(tap_p.at[to], tap_r.at[y], tsend.at[0, dy - 1], trecv.at[0, y], ydev(dy))

    for dy in range(1, NY):
        tap_scatter(dy).start()

    def a_copy(dy):
        block = rows(y * TOK, TOK)
        return rcopy(ag.at[block], ag.at[block], asend.at[dy - 1], arecv.at[y], ydev(dy))

    @pl.when(active)
    def _():
        for dy in range(1, NY):
            a_copy(dy).start()
        ring_go(2)

    tap_r[y] = tap_p[y]
    for dy in range(1, NY):
        wait_in(tap_r.at[(y + dy) % NY], trecv.at[0, (y + dy) % NY])
    tap_s[...] = (tap_r[0] + tap_r[1]) + (tap_r[2] + tap_r[3])

    def tap_gather(dz):
        return rcopy(tap_s, tap_z.at[z], tsend.at[1, dz - 1], trecv.at[1, z], zdev(dz))

    for dz in range(1, NZ):
        tap_gather(dz).start()

    def back(src, half):
        return rcopy(
            yout.at[half, rows(src * CAP, CAP)],
            ret.at[rows(me * CAP, CAP)],
            ysend.at[src, half], yrecv.at[me],
            (sec - 1, core * 16 + src, half),
        )

    def expert_chunk(turn):
        zs = (turn + z) % 4
        block = rows(zs * 64, 64)

        def arrive(i, carry):
            src = zs * NY + i // 2
            wait_in(xin.at[i % 2, rows(src * CAP, CAP)], xrecv.at[src, i % 2])
            return carry

        lax.fori_loop(0, 8, arrive, 0)
        if turn == 0:
            own_down.wait()
            wait_in(wdn.at[other], wrecv.at[0])
            own_pre.wait()
            wait_in(prev_.at[other], wrecv.at[2])
        x0 = xin[0, block, :]
        x1 = xin[1, block, :]
        grads = []
        for h in range(2):
            hidden = dot_nt(x0, wdn[h, :, 0:HALF]) + dot_nt(x1, wdn[h, :, HALF:])
            slope = silu_slope(prev_[h, block, :].astype(F32))
            grads.append((hidden * slope).astype(BF16))
        if turn == 0:
            own_up.wait()
            wait_in(wup.at[other], wrecv.at[1])
        for half in range(2):
            @pl.loop(0, 4)
            def _(t):
                wide = pl.ds(pl.multiple_of(half * HALF + t * 512, 512), 512)
                cols = pl.ds(pl.multiple_of(t * 512, 512), 512)
                value = dot_nt(grads[0], wup[0, wide, :]) + dot_nt(grads[1], wup[1, wide, :])
                yout[half, block, cols] = value.astype(BF16)

        def give(i, carry):
            back(zs * NY + (y + i // 2) % NY, i % 2).start()
            return carry

        lax.fori_loop(0, 8, give, 0)

    @pl.when(active)
    def _():
        expert_chunk(0)
        ring_go(3)
        expert_chunk(1)
        ring_go(4)
        expert_chunk(2)

    tap_z[z] = tap_s[...]
    for dz in range(1, NZ):
        wait_in(tap_z.at[(z + dz) % NZ], trecv.at[1, (z + dz) % NZ])
    total = tap_z[0]
    for i in range(1, NZ):
        total = total + tap_z[i]
    tap_t[...] = total

    def tap_share(dy):
        return rcopy(tap_t, tap_o.at[y], tsend.at[2, dy - 1], trecv.at[2, y], ydev(dy))

    for dy in range(1, NY):
        tap_share(dy).start()

    give_part = rcopy(part.at[other], part_r, psem_s.at[0], psem_r.at[0], partner)

    def proj_back(to):
        return rcopy(psend.at[to], prec.at[y], qsend.at[to], qrecv.at[y], (sec - 1, z * NY + to, core))

    @pl.when(active)
    def _():
        expert_chunk(3)
        for dy in range(1, NY):
            wait_in(ag.at[rows(((y + dy) % NY) * TOK, TOK)], arecv.at[(y + dy) % NY])
        ring_arrived(4)
        own_rows.wait()

        def product(h):
            @pl.loop(0, 4)
            def _(i):
                tokens = pl.ds(pl.multiple_of((i // 2) * 256, 256), 256)
                cols = pl.ds(pl.multiple_of((i % 2) * 256, 256), 256)
                wide = pl.ds(pl.multiple_of(h * 512 + (i % 2) * 256, 256), 256)
                part[h, tokens, cols] = dot_nt(ag[tokens, :], bg[wide, :])

        product(other)
        give_part.start()
        product(core)
        wait_in(part_r, psem_r.at[0])
        for to in range(NY):
            tokens = pl.ds(to * TOK, TOK)
            psend[to] = (part[core, tokens, :] + part_r[tokens, :]).astype(BF16)
        for to in range(NY):
            proj_back(to).start()

    @pl.when(sec < NSEC - 1)
    def _():
        wait_in(og_r, orecv.at[0])
        wait_in(comb_r, orecv.at[1])
        for i in range(NY):
            wait_in(prec.at[i], qrecv.at[i])

        def arrive(i, carry):
            wait_in(ret.at[rows(i * CAP, CAP)], yrecv.at[i])
            return carry

        lax.fori_loop(0, NEXP, arrive, 0)
        for tile in range(4):
            cols = pl.ds(tile * 512, 512)
            proj = jnp.concatenate([prec[i, :, tile * 128 : tile * 128 + 128] for i in range(NY)], axis=1)
            moe = jnp.dot(comb_r[...], ret[:, cols], preferred_element_type=F32)
            out[:, cols] = (og_r[:, cols].astype(F32) + moe + proj.astype(F32)).astype(BF16)

    @pl.when(sec == NSEC - 1)
    def _():
        out[...] = jnp.zeros_like(out)

    tap_o[y] = tap_t[...]
    for dy in range(1, NY):
        wait_in(tap_o.at[(y + dy) % NY], trecv.at[2, (y + dy) % NY])
    for quarter in range(4):
        kout[:, pl.ds(quarter * 512, 512)] = tap_o[quarter, 0:4, :]

    @pl.when(has_prev)
    def _():
        halo_g_out.wait_send()

    @pl.when(has_next)
    def _():
        halo_i_out.wait_send()

    for dy in range(1, NY):
        tap_scatter(dy).wait_send()
        tap_share(dy).wait_send()
    for dz in range(1, NZ):
        tap_gather(dz).wait_send()

    @pl.when(active)
    def _():
        for step in range(1, 5):
            ring(step, True).wait_send()
            ring(step, False).wait_send()
        for dy in range(1, NY):
            a_copy(dy).wait_send()
        give_down.wait_send()
        give_up.wait_send()
        give_pre.wait_send()
        give_og.wait_send()
        give_comb.wait_send()
        give_part.wait_send()
        for to in range(NY):
            proj_back(to).wait_send()

        def sent(e, carry):
            own = (e == me) & (mine == core)

            @pl.when(jnp.logical_not(own))
            def _():
                block_copy(e).wait_send()

            back(e // 2, e % 2).wait_send()
            return carry

        lax.fori_loop(0, NEXP, sent, 0)


def shards(
    out_grad, expert_ids, gate_codes, up_weight, down_weight, pre_act, conv_grad, conv_input, conv_weight, in_proj
):
    vmem = pl.BlockSpec(memory_space=pltpu.VMEM)
    anywhere = pl.BlockSpec(memory_space=pl.ANY)
    dma = pltpu.SemaphoreType.DMA
    out, kout = pl.pallas_call(
        kernel,
        out_shape=(
            jax.ShapeDtypeStruct((TOK, HALF), BF16),
            jax.ShapeDtypeStruct((4, HALF), F32),
        ),
        in_specs=[vmem] * 7 + [anywhere] * 3,
        out_specs=(vmem, vmem),
        scratch_shapes=[
            pltpu.VMEM((2, 512, 4096), BF16),
            pltpu.VMEM((2, 4096, 512), BF16),
            pltpu.VMEM((2, 256, 512), BF16),
            pltpu.VMEM((512, HALF), BF16),
            pltpu.VMEM((2, 256, HALF), BF16),
            pltpu.VMEM((2, 256, HALF), BF16),
            pltpu.VMEM((512, HALF), BF16),
            pltpu.VMEM((TOK, 512), BF16),
            pltpu.VMEM((TOK, 512), BF16),
            pltpu.VMEM((TOK, HALF), BF16),
            pltpu.VMEM((NZ * TOK, HALF), BF16),
            pltpu.VMEM((NY * TOK, HALF), BF16),
            pltpu.VMEM((16, HALF), BF16),
            pltpu.VMEM((16, HALF), BF16),
            pltpu.VMEM((TOK + 8, HALF), F32),
            pltpu.VMEM((TOK + 8, HALF), F32),
            pltpu.VMEM((2, 512, 512), F32),
            pltpu.VMEM((512, 512), F32),
            pltpu.VMEM((NY, TOK, 512), BF16),
            pltpu.VMEM((NY, TOK, 512), BF16),
            pltpu.VMEM((NY, 8, 512), F32),
            pltpu.VMEM((NY, 8, 512), F32),
            pltpu.VMEM((8, 512), F32),
            pltpu.VMEM((NZ, 8, 512), F32),
            pltpu.VMEM((8, 512), F32),
            pltpu.VMEM((NY, 8, 512), F32),
            dma((5,)),
            dma((3,)), dma((3,)),
            dma((2,)), dma((2,)),
            dma((2,)), dma((2,)),
            dma((4, 2)), dma((4, 2)),
            dma((NEXP,)), dma((16, 2)),
            dma((16, 2)), dma((NEXP,)),
            dma((3,)), dma((NY,)),
            dma((1,)), dma((1,)),
            dma((NY,)), dma((NY,)),
            dma((3, 7)), dma((3, NZ)),
        ],
        compiler_params=pltpu.CompilerParams(has_side_effects=True, vmem_limit_bytes=60 * 1024 * 1024),
        name="layer_backward",
    )(
        out_grad[0], expert_ids[0], gate_codes[0], conv_grad[0], conv_input[0], conv_weight[0], in_proj[0],
        up_weight[0, 0], down_weight[0, 0], pre_act[0, 0],
    )
    return out[None], kout[None]


def solution(mesh):
    in_specs = (
        P("section", "expert", "mp"),
        P("section", "expert", None),
        P("section", "expert", None),
        P("section", "expert", None, "mp"),
        P("section", "expert", "mp", None),
        P("section", "expert", None, "mp"),
        P("section", "expert", "mp"),
        P("section", "expert", "mp"),
        P("section", None, "mp"),
        P("section", "expert", "mp"),
    )
    out_specs = (P("section", "expert", "mp"), P("section", None, "mp"))
    return jax.shard_map(shards, mesh=mesh, in_specs=in_specs, out_specs=out_specs, check_vma=False)
```

```python
import jax
import jax.numpy as jnp
from jax import lax
from jax.experimental import pallas as pl
from jax.experimental.pallas import tpu as pltpu
from jax.sharding import PartitionSpec as P

MESH = pl.DeviceIdType.MESH
F32 = jnp.float32
BF16 = jnp.bfloat16

NY = 4
NZ = 8
CAP = 16
TOK = 128
HALF = 2048
NSEC = 4
NEXP = 32
SPREAD = 2
CHUNK = 2048 // SPREAD
WIDE = CHUNK + 2 * HALF
NT = (((1,), (1,)), ((), ()))


def dot_nt(a, b):
    return lax.dot_general(a, b, NT, preferred_element_type=F32)


def silu_slope(pre_value):
    sig = 1.0 / (1.0 + jnp.exp(-pre_value))
    return sig * (1.0 + pre_value * (1.0 - sig))


def kernel(
    og, ids, codes, cg, ci, cw, bp, up, down, pre,
    out, kout,
    wdn, wup, prev_, sbuf, xin, yout, ret, comb, res,
    bg, ag, gin, cwin, halo_i, gext, iext, psend, prec, base,
    tap_p, tap_r, tap_s, tap_z, tap_t, tap_o,
    lsem, wsend, wrecv, hsend, hrecv, osend, orecv,
    bsend, brecv, xsend, xrecv, ysend, yrecv, asend, arecv,
    jsend, jrecv, qsend, qrecv, tsend, trecv,
):
    sec = lax.axis_index("section")
    me = lax.axis_index("expert")
    core = lax.axis_index("mp")
    z = me // NY
    y = me % NY
    mine = z // 4
    other = 1 - core
    partner = (sec, me, other)

    def rcopy(src, dst, ssem, rsem, dev):
        return pltpu.make_async_remote_copy(
            src_ref=src, dst_ref=dst, send_sem=ssem, recv_sem=rsem,
            device_id=dev, device_id_type=MESH,
        )

    def wait_in(dst, rsem):
        rcopy(dst, dst, lsem.at[0], rsem, partner).wait_recv()

    def wait_out(src, ssem):
        rcopy(src, src, ssem, lsem.at[0], partner).wait_send()

    def zdev(dz):
        return (sec, ((z + dz + NZ) % NZ) * NY + y, core)

    def ydev(dy):
        return (sec, z * NY + (y + dy) % NY, core)

    def rows(start, size):
        return pl.ds(pl.multiple_of(start, size), size)

    has_next = me < NEXP - 1
    has_prev = me > 0
    active = sec > 0
    fed = sec < NSEC - 1

    barrier = pltpu.get_barrier_semaphore()

    def greet(i, carry):
        pl.semaphore_signal(
            barrier, inc=1, device_id=(sec, (me + i // 2) % NEXP, (core + i) % 2), device_id_type=MESH
        )
        return carry

    lax.fori_loop(1, 2 * NEXP, greet, 0)

    def greet_far(i, carry):
        there = ((sec + 1 + i // 8) % NSEC, z * NY + (i // 2) % NY, i % 2)
        pl.semaphore_signal(barrier, inc=1, device_id=there, device_id_type=MESH)
        return carry

    lax.fori_loop(0, 24, greet_far, 0)

    def greet_side(i, carry):
        side = me + 2 * (i % 2) - 1

        @pl.when((side >= 0) & (side < NEXP))
        def _():
            there = ((sec + 1 + i // 4) % NSEC, side, (i // 2) % 2)
            pl.semaphore_signal(barrier, inc=1, device_id=there, device_id_type=MESH)

        return carry

    lax.fori_loop(0, 12, greet_side, 0)

    halo_i_out = rcopy(ci.at[pl.ds(TOK - 16, 16)], halo_i, hsend.at[1], hrecv.at[1], (sec, me + 1, core))

    JOBS = ((2, 0, CHUNK), (1, CHUNK, HALF), (3, CHUNK + HALF, HALF))
    runs = sec >= NSEC - SPREAD

    def job_cols(job):
        return pl.ds(JOBS[job][1], JOBS[job][2])

    def ring(job, step, up_way):
        shard = (z - (step - 1) + NZ) % NZ if up_way else (z + (step - 1)) % NZ
        way = 0 if up_way else 1
        start, size = (0, TOK) if step < 4 else ((0, 64) if up_way else (64, 64))
        block = bg.at[pl.ds(pl.multiple_of(shard * TOK + start, 64), size), job_cols(job)]
        return rcopy(
            block, block, bsend.at[job, step - 1, way], brecv.at[job, step - 1, way], zdev(1 if up_way else -1)
        )

    def ring_arrived(job, step):
        for way in range(2):
            shard = (z - step + NZ) % NZ if way == 0 else (z + step) % NZ
            start, size = (0, TOK) if step < 4 else ((0, 64) if way == 0 else (64, 64))
            block = pl.ds(pl.multiple_of(shard * TOK + start, 64), size)
            wait_in(bg.at[block, job_cols(job)], brecv.at[job, step - 1, way])

    def ring_go(job, step):
        if step == 1:
            wait_in(bg.at[rows(z * TOK, TOK), job_cols(job)], jrecv.at[job, 0])
        else:
            ring_arrived(job, step - 1)
        ring(job, step, True).start()
        ring(job, step, False).start()

    def slice_of(i):
        piece = core * SPREAD + i
        return pl.ds(i * CHUNK, CHUNK), 3 - piece // 2, piece % 2

    def gifts(job, i):
        if job == 0:
            cols, to, half = slice_of(i)
        else:
            cols, to, half = pl.ds(0, HALF), 0, core
        there = job_cols(job)
        return (
            rcopy(bp.at[:, cols], bg.at[rows(z * TOK, TOK), there], jsend.at[i, 0], jrecv.at[job, 0], (to, me, half)),
            rcopy(cg.at[:, cols], gin.at[pl.ds(0, TOK), there], jsend.at[i, 1], jrecv.at[job, 1], (to, me, half)),
            rcopy(cw.at[:, cols], cwin.at[:, there], jsend.at[i, 2], jrecv.at[job, 2], (to, me, half)),
            rcopy(
                cg.at[pl.ds(0, 16), cols], gin.at[pl.ds(TOK, 16), there], jsend.at[i, 3], jrecv.at[job, 3],
                (to, me - 1, half),
            ),
        )

    def gifts_here():
        cols, there = pl.ds(CHUNK, CHUNK), job_cols(0)
        return (
            pltpu.make_async_copy(bp.at[:, cols], bg.at[rows(z * TOK, TOK), there], jrecv.at[0, 0]),
            pltpu.make_async_copy(cg.at[:, cols], gin.at[pl.ds(0, TOK), there], jrecv.at[0, 1]),
            pltpu.make_async_copy(cw.at[:, cols], cwin.at[:, there], jrecv.at[0, 2]),
        )

    def share(act, local):
        def some(copies, kinds):
            for kind in kinds:
                act(copies[kind])

        for job in (1, 2):
            @pl.when(sec == JOBS[job][0])
            def _():
                some(gifts(job, 0), (0, 1, 2))

                @pl.when(has_prev)
                def _():
                    some(gifts(job, 0), (3,))

        @pl.when(sec == 2)
        def _():
            for i in range(SPREAD):
                if i == 1:
                    @pl.when(core == 0)
                    def _():
                        some(gifts(0, 1), (0, 1, 2))

                    if local:
                        @pl.when(core == 1)
                        def _():
                            for copy in gifts_here():
                                copy.start()
                else:
                    some(gifts(0, i), (0, 1, 2))

                @pl.when(has_prev)
                def _():
                    some(gifts(0, i), (3,))

    def conv(job):
        there, width = job_cols(job), JOBS[job][2]
        wait_in(gin.at[pl.ds(0, TOK), there], jrecv.at[job, 1])
        wait_in(cwin.at[:, there], jrecv.at[job, 2])

        @pl.when(has_next)
        def _():
            wait_in(gin.at[pl.ds(TOK, 16), there], jrecv.at[job, 3])
            gext[pl.ds(TOK, 8), pl.ds(0, width)] = gin[pl.ds(TOK, 16), there].astype(F32)[0:8]

        @pl.when(jnp.logical_not(has_next))
        def _():
            gext[pl.ds(TOK, 8), pl.ds(0, width)] = jnp.zeros((8, width), F32)

        gext[pl.ds(0, TOK), pl.ds(0, width)] = gin[pl.ds(0, TOK), there].astype(F32)

        @pl.loop(0, width // 128)
        def _(i):
            lanes = pl.ds(pl.multiple_of(i * 128, 128), 128)
            cols = pl.ds(pl.multiple_of(JOBS[job][1] + i * 128, 128), 128)
            total = jnp.zeros((TOK, 128), F32)
            for tap in range(4):
                total = total + cwin[tap : tap + 1, cols] * gext[pl.ds(3 - tap, TOK), lanes]
            ag[rows(y * TOK, TOK), cols] = total.astype(BF16)

        for dy in range(1, NY):
            a_copy(job, dy).start()

    def a_copy(job, dy):
        block = ag.at[rows(y * TOK, TOK), job_cols(job)]
        return rcopy(block, block, asend.at[job, dy - 1], arecv.at[job, y], ydev(dy))

    place = (NSEC - 1 - sec) * 2 + core

    def product(job, shard):
        col, width = JOBS[job][1], JOBS[job][2]
        tall = rows(shard * TOK, TOK)
        psend[job, shard] = dot_nt(ag[:, pl.ds(col, width)], bg[tall, pl.ds(col, width)]).astype(BF16)

    def proj_back(job, shard, dy):
        to = (y + dy) % NY
        half = shard // 4
        which = place if job == 0 else core
        return rcopy(
            psend.at[job, shard, rows(to * TOK, TOK)],
            prec.at[which, y, :, rows((shard % 4) * TOK, TOK)],
            qsend.at[job, shard, 0 if dy == 0 else 1], qrecv.at[which, y],
            (JOBS[job][0], z * NY + to, half),
        )

    def proj_local(job, shard):
        return (sec == 2) & (shard // 4 == core) if job == 0 else sec == NSEC

    def proj_go(job, shard):
        product(job, shard)
        for dy in range(1, NY):
            proj_back(job, shard, dy).start()
        if job == 0:
            here = proj_local(job, shard)

            @pl.when(here)
            def _():
                prec[place, y, :, rows((shard % 4) * TOK, TOK)] = psend[job, shard, rows(y * TOK, TOK), :]

            @pl.when(jnp.logical_not(here))
            def _():
                proj_back(job, shard, 0).start()
        else:
            proj_back(job, shard, 0).start()

    def proj_sent(job):
        def one(shard, carry):
            wait_out(psend.at[job, shard, pl.ds(0, 3 * TOK)], qsend.at[job, shard, 1])
            if job == 0:
                @pl.when(jnp.logical_not(proj_local(job, shard)))
                def _():
                    proj_back(job, shard, 0).wait_send()
            else:
                proj_back(job, shard, 0).wait_send()
            return carry

        lax.fori_loop(0, NZ, one, 0)

    def proj_step(job, step):
        def one(i, carry):
            shard = (z - step + NZ) % NZ + i * ((z + step) % NZ - (z - step + NZ) % NZ)
            proj_go(job, shard)
            return carry

        lax.fori_loop(0, 1 if step in (0, 4) else 2, one, 0)

    def tokens_arrived(job):
        for dy in range(1, NY):
            i = (y + dy) % NY
            wait_in(ag.at[rows(i * TOK, TOK), job_cols(job)], arecv.at[job, i])

    own_down = pltpu.make_async_copy(down, wdn.at[core], lsem.at[1])
    own_up = pltpu.make_async_copy(up, wup.at[core], lsem.at[2])
    own_pre = pltpu.make_async_copy(pre.at[rows(core * 256, 256)], prev_.at[core], lsem.at[3])
    give_down = rcopy(down, wdn.at[core], wsend.at[0], wrecv.at[0], partner)
    give_up = rcopy(up, wup.at[core], wsend.at[1], wrecv.at[1], partner)
    give_pre = rcopy(pre.at[rows(other * 256, 256)], prev_.at[core], wsend.at[2], wrecv.at[2], partner)
    def block_copy(e):
        return rcopy(
            sbuf.at[rows(e * CAP, CAP)],
            xin.at[core, rows((me % 16) * CAP, CAP)],
            xsend.at[e], xrecv.at[me % 16, core], (sec, e, mine),
        )

    def block_local(e):
        return pltpu.make_async_copy(
            sbuf.at[rows(e * CAP, CAP)],
            xin.at[core, rows((me % 16) * CAP, CAP)],
            xrecv.at[me % 16, core],
        )

    @pl.when(active)
    def _():
        own_down.start()
        own_up.start()
        own_pre.start()

        line = lax.broadcasted_iota(jnp.int32, (NEXP * CAP, TOK), 0)
        expert = line // CAP
        rank = line % CAP
        first = ids[0:1, :] == expert
        second = ids[1:2, :] == expert
        named = first | second
        gates = codes[...].astype(F32) / 256.0
        gate = jnp.where(first, gates[0:1, :], 0.0) + jnp.where(second, gates[1:2, :], 0.0)
        low = lax.broadcasted_iota(jnp.int32, (TOK, TOK), 0) < lax.broadcasted_iota(jnp.int32, (TOK, TOK), 1)
        before = jnp.dot(
            jnp.where(named, 1.0, 0.0).astype(BF16),
            jnp.where(low, 1.0, 0.0).astype(BF16),
            preferred_element_type=F32,
        )
        here = named & (before == rank.astype(F32))
        placed = jnp.where(here, gate, 0.0).astype(BF16)
        for tile in range(4):
            cols = pl.ds(tile * 512, 512)
            sbuf[:, cols] = jnp.dot(placed, og[:, cols], preferred_element_type=F32).astype(BF16)
        comb[...] = jnp.where(here, 1.0, 0.0).T.astype(BF16)

    pl.semaphore_wait(barrier, 2 * NEXP - 1 + 24 + 6 * has_prev.astype(jnp.int32) + 6 * has_next.astype(jnp.int32))

    @pl.when(has_next)
    def _():
        halo_i_out.start()

    share(lambda copy: copy.start(), True)

    def dispatch(first_turn, turns):
        def send_block(i, carry):
            turn = i // 8
            zt = (z - turn + 8) % 4 + 4 * ((i // 4) % 2)
            e = zt * NY + (y + i) % NY
            own = (e == me) & (mine == core)

            @pl.when(own)
            def _():
                block_local(e).start()

            @pl.when(jnp.logical_not(own))
            def _():
                block_copy(e).start()

            return carry

        lax.fori_loop(first_turn * 8, (first_turn + turns) * 8, send_block, 0)

    both = active & runs

    @pl.when(both)
    def _():
        ring_go(0, 1)
        dispatch(0, 1)

    @pl.when(active & jnp.logical_not(runs))
    def _():
        dispatch(0, 4)

    @pl.when(active)
    def _():
        give_down.start()
        give_pre.start()
        give_up.start()

    @pl.when(jnp.logical_not(active))
    def _():
        ring_go(1, 1)
        ring_go(2, 1)

    @pl.when(has_prev)
    def _():
        wait_in(halo_i, hrecv.at[1])

    @pl.when(jnp.logical_not(has_prev))
    def _():
        halo_i[...] = jnp.zeros_like(halo_i)

    iext[pl.ds(0, 8), :] = halo_i[...].astype(F32)[8:16]
    iext[pl.ds(8, TOK), :] = ci[...].astype(F32)
    tap_p[...] = jnp.zeros_like(tap_p)

    for quarter in range(4):
        @pl.loop(0, 4)
        def _(i):
            cols = pl.ds(pl.multiple_of(quarter * 512 + i * 128, 128), 128)
            lanes = pl.ds(pl.multiple_of(i * 128, 128), 128)
            grad = cg[:, cols].astype(F32)
            for tap in range(4):
                term = grad * iext[pl.ds(5 + tap, TOK), cols]
                tap_p[quarter, tap : tap + 1, lanes] = jnp.sum(term, axis=0, keepdims=True)

    def tap_scatter(dy):
        to = (y + dy) % NY
        return rcopy(tap_p.at[to], tap_r.at[y], tsend.at[0, dy - 1], trecv.at[0, y], ydev(dy))

    for dy in range(1, NY):
        tap_scatter(dy).start()

    @pl.when(runs)
    def _():
        conv(0)

    @pl.when(jnp.logical_not(active))
    def _():
        conv(1)
        conv(2)
        for job in (1, 2):
            ring_go(job, 2)

    @pl.when(both)
    def _():
        ring_go(0, 2)
        dispatch(1, 1)
        ring_go(0, 3)
        dispatch(2, 1)

    tap_r[y] = tap_p[y]
    for dy in range(1, NY):
        wait_in(tap_r.at[(y + dy) % NY], trecv.at[0, (y + dy) % NY])
    tap_s[...] = (tap_r[0] + tap_r[1]) + (tap_r[2] + tap_r[3])

    def tap_gather(dz):
        return rcopy(tap_s, tap_z.at[z], tsend.at[1, dz - 1], trecv.at[1, z], zdev(dz))

    for dz in range(1, NZ):
        tap_gather(dz).start()

    def back(src, half):
        return rcopy(
            yout.at[half, rows(src * CAP, CAP)],
            ret.at[rows(me * CAP, CAP)],
            ysend.at[src, half], yrecv.at[me],
            (sec, core * 16 + src, half),
        )

    def back_local(src):
        return pltpu.make_async_copy(
            yout.at[core, rows(src * CAP, CAP)], ret.at[rows(me * CAP, CAP)], yrecv.at[me]
        )

    def expert_chunk(turn):
        zs = (turn + z) % 4
        block = rows(zs * 64, 64)

        def arrive(i, carry):
            src = zs * NY + i // 2
            wait_in(xin.at[i % 2, rows(src * CAP, CAP)], xrecv.at[src, i % 2])
            return carry

        lax.fori_loop(0, 8, arrive, 0)
        if turn == 0:
            own_down.wait()
            wait_in(wdn.at[other], wrecv.at[0])
            own_pre.wait()
            wait_in(prev_.at[other], wrecv.at[2])
        x0 = xin[0, block, :]
        x1 = xin[1, block, :]
        grads = []
        for h in range(2):
            hidden = dot_nt(x0, wdn[h, :, 0:HALF]) + dot_nt(x1, wdn[h, :, HALF:])
            slope = silu_slope(prev_[h, block, :].astype(F32))
            grads.append((hidden * slope).astype(BF16))
        if turn == 0:
            own_up.wait()
            wait_in(wup.at[other], wrecv.at[1])
        for half in range(2):
            @pl.loop(0, 4)
            def _(t):
                wide = pl.ds(pl.multiple_of(half * HALF + t * 512, 512), 512)
                cols = pl.ds(pl.multiple_of(t * 512, 512), 512)
                value = dot_nt(grads[0], wup[0, wide, :]) + dot_nt(grads[1], wup[1, wide, :])
                yout[half, block, cols] = value.astype(BF16)

        def give(i, carry):
            src = zs * NY + (y + i // 2) % NY
            own = (core * 16 + src == me) & (i % 2 == core)

            @pl.when(own)
            def _():
                back_local(src).start()

            @pl.when(jnp.logical_not(own))
            def _():
                back(src, i % 2).start()

            return carry

        lax.fori_loop(0, 8, give, 0)

    @pl.when(active)
    def _():
        expert_chunk(0)

        @pl.when(runs)
        def _():
            ring_go(0, 4)
            dispatch(3, 1)

        expert_chunk(1)
        expert_chunk(2)

        @pl.when(runs)
        def _():
            tokens_arrived(0)
            for step in range(4):
                proj_step(0, step)
            ring_arrived(0, 4)
            proj_step(0, 4)

    @pl.when(jnp.logical_not(active))
    def _():
        for job in (1, 2):
            ring_go(job, 3)
        for job in (1, 2):
            tokens_arrived(job)
            proj_step(job, 0)
            proj_step(job, 1)
        for job in (1, 2):
            ring_go(job, 4)
        for job in (1, 2):
            proj_step(job, 2)
            proj_step(job, 3)
        for job in (1, 2):
            ring_arrived(job, 4)
            proj_step(job, 4)

    tap_z[z] = tap_s[...]
    for dz in range(1, NZ):
        wait_in(tap_z.at[(z + dz) % NZ], trecv.at[1, (z + dz) % NZ])
    total = tap_z[0]
    for i in range(1, NZ):
        total = total + tap_z[i]
    tap_t[...] = total

    def tap_share(dy):
        return rcopy(tap_t, tap_o.at[y], tsend.at[2, dy - 1], trecv.at[2, y], ydev(dy))

    for dy in range(1, NY):
        tap_share(dy).start()

    def result_out(tile):
        cols = pl.ds(tile * 512, 512)
        return rcopy(res.at[:, cols], out.at[:, cols], osend.at[tile], orecv.at[tile], (sec - 1, me, core))

    @pl.when(active)
    def _():
        expert_chunk(3)

    @pl.when(active)
    def _():
        def partial(which, carry):
            for i in range(NY):
                own = (sec == 2) & (which == place) & (i == y)

                @pl.when(jnp.logical_not(own))
                def _():
                    wait_in(prec.at[which, i], qrecv.at[which, i])

            for i in range(NY):
                for tile in range(4):
                    cols = pl.ds((tile * NY + i) * TOK, TOK)
                    base[:, cols] += prec[which, i, :, pl.ds(tile * TOK, TOK)].astype(F32)
            return carry

        base[...] = og[...].astype(F32)
        lax.fori_loop(0, jnp.where(sec == 2, 2 * SPREAD, 2), partial, 0)

        def arrive(i, carry):
            wait_in(ret.at[rows(i * CAP, CAP)], yrecv.at[i])
            return carry

        lax.fori_loop(0, NEXP, arrive, 0)
        for tile in range(4):
            cols = pl.ds(tile * 512, 512)
            moe = jnp.dot(comb[...], ret[:, cols], preferred_element_type=F32)
            res[:, cols] = (base[:, cols] + moe).astype(BF16)
            result_out(tile).start()

    @pl.when(fed)
    def _():
        for tile in range(4):
            wait_in(out.at[:, pl.ds(tile * 512, 512)], orecv.at[tile])

    @pl.when(jnp.logical_not(fed))
    def _():
        out[...] = jnp.zeros_like(out)

    tap_o[y] = tap_t[...]
    for dy in range(1, NY):
        wait_in(tap_o.at[(y + dy) % NY], trecv.at[2, (y + dy) % NY])
    for quarter in range(4):
        kout[:, pl.ds(quarter * 512, 512)] = tap_o[quarter, 0:4, :]

    share(lambda copy: copy.wait_send(), False)

    def ring_sent(job):
        for step in range(1, 5):
            ring(job, step, True).wait_send()
            ring(job, step, False).wait_send()
        for dy in range(1, NY):
            a_copy(job, dy).wait_send()
        proj_sent(job)

    @pl.when(runs)
    def _():
        ring_sent(0)

    @pl.when(jnp.logical_not(active))
    def _():
        ring_sent(1)
        ring_sent(2)

    @pl.when(has_next)
    def _():
        halo_i_out.wait_send()

    for dy in range(1, NY):
        tap_scatter(dy).wait_send()
        tap_share(dy).wait_send()
    for dz in range(1, NZ):
        tap_gather(dz).wait_send()

    @pl.when(active)
    def _():
        give_down.wait_send()
        give_up.wait_send()
        give_pre.wait_send()
        for tile in range(4):
            result_out(tile).wait_send()

        def sent(e, carry):
            own = (e == me) & (mine == core)

            @pl.when(jnp.logical_not(own))
            def _():
                block_copy(e).wait_send()

            mirror = (core * 16 + e // 2 == me) & (e % 2 == core)

            @pl.when(jnp.logical_not(mirror))
            def _():
                back(e // 2, e % 2).wait_send()

            return carry

        lax.fori_loop(0, NEXP, sent, 0)


def shards(
    out_grad, expert_ids, gate_codes, up_weight, down_weight, pre_act, conv_grad, conv_input, conv_weight, in_proj
):
    vmem = pl.BlockSpec(memory_space=pltpu.VMEM)
    anywhere = pl.BlockSpec(memory_space=pl.ANY)
    dma = pltpu.SemaphoreType.DMA
    out, kout = pl.pallas_call(
        kernel,
        out_shape=(
            jax.ShapeDtypeStruct((TOK, HALF), BF16),
            jax.ShapeDtypeStruct((4, HALF), F32),
        ),
        in_specs=[vmem] * 7 + [anywhere] * 3,
        out_specs=(vmem, vmem),
        scratch_shapes=[
            pltpu.VMEM((2, 512, 4096), BF16),
            pltpu.VMEM((2, 4096, 512), BF16),
            pltpu.VMEM((2, 256, 512), BF16),
            pltpu.VMEM((512, HALF), BF16),
            pltpu.VMEM((2, 256, HALF), BF16),
            pltpu.VMEM((2, 256, HALF), BF16),
            pltpu.VMEM((512, HALF), BF16),
            pltpu.VMEM((TOK, 512), BF16),
            pltpu.VMEM((TOK, HALF), BF16),
            pltpu.VMEM((NZ * TOK, WIDE), BF16),
            pltpu.VMEM((NY * TOK, WIDE), BF16),
            pltpu.VMEM((TOK + 16, WIDE), BF16),
            pltpu.VMEM((4, WIDE), F32),
            pltpu.VMEM((16, HALF), BF16),
            pltpu.VMEM((TOK + 8, HALF), F32),
            pltpu.VMEM((TOK + 8, HALF), F32),
            pltpu.VMEM((3, NZ, NY * TOK, TOK), BF16),
            pltpu.VMEM((2 * SPREAD, NY, TOK, 512), BF16),
            pltpu.VMEM((TOK, HALF), F32),
            pltpu.VMEM((NY, 8, 512), F32),
            pltpu.VMEM((NY, 8, 512), F32),
            pltpu.VMEM((8, 512), F32),
            pltpu.VMEM((NZ, 8, 512), F32),
            pltpu.VMEM((8, 512), F32),
            pltpu.VMEM((NY, 8, 512), F32),
            dma((5,)),
            dma((3,)), dma((3,)),
            dma((2,)), dma((2,)),
            dma((4,)), dma((4,)),
            dma((3, 4, 2)), dma((3, 4, 2)),
            dma((NEXP,)), dma((16, 2)),
            dma((16, 2)), dma((NEXP,)),
            dma((3, 3)), dma((3, NY)),
            dma((SPREAD, 4)), dma((3, 4)),
            dma((3, NZ, 2)), dma((2 * SPREAD, NY)),
            dma((3, 7)), dma((3, NZ)),
        ],
        compiler_params=pltpu.CompilerParams(has_side_effects=True, collective_id=0, vmem_limit_bytes=63 * 1024 * 1024),
        name="layer_backward",
    )(
        out_grad[0], expert_ids[0].T, gate_codes[0].T, conv_grad[0], conv_input[0], conv_weight[0], in_proj[0],
        up_weight[0, 0], down_weight[0, 0], pre_act[0, 0],
    )
    return out[None], kout[None]


def solution(mesh):
    in_specs = (
        P("section", "expert", "mp"),
        P("section", "expert", None),
        P("section", "expert", None),
        P("section", "expert", None, "mp"),
        P("section", "expert", "mp", None),
        P("section", "expert", None, "mp"),
        P("section", "expert", "mp"),
        P("section", "expert", "mp"),
        P("section", None, "mp"),
        P("section", "expert", "mp"),
    )
    out_specs = (P("section", "expert", "mp"), P("section", None, "mp"))
    return jax.shard_map(shards, mesh=mesh, in_specs=in_specs, out_specs=out_specs, check_vma=False)
```

```python
import jax
import jax.numpy as jnp
from jax import lax
from jax.experimental import pallas as pl
from jax.experimental.pallas import tpu as pltpu
from jax.sharding import PartitionSpec as P

MESH = pl.DeviceIdType.MESH
F32 = jnp.float32
BF16 = jnp.bfloat16

NY = 4
NZ = 8
CAP = 16
TOK = 128
HALF = 2048
NSEC = 4
NEXP = 32
SPREAD = 2
CHUNK = 2048 // SPREAD
WIDE = CHUNK + 2 * HALF
NT = (((1,), (1,)), ((), ()))


def dot_nt(a, b):
    return lax.dot_general(a, b, NT, preferred_element_type=F32)


def silu_slope(pre_value):
    sig = 1.0 / (1.0 + jnp.exp(-pre_value))
    return sig * (1.0 + pre_value * (1.0 - sig))


def kernel(
    og, ids, codes, cg, ci, cw, bp, up, down, pre,
    out, kout,
    wdn, wup, prev_, sbuf, xin, yout, ret, comb, combt, res, part_in, ret_late, comb_late,
    bg, ag, gin, cwin, halo_i, gext, iext, psend, pin, prec, base,
    tap_p, tap_r, tap_s, tap_z, tap_t, tap_o,
    lsem, wsend, wrecv, hsend, hrecv, osend, orecv,
    bsend, brecv, xsend, xrecv, ysend, yrecv, asend, arecv,
    jsend, jrecv, lsend, lrecv, csend, crecv, esend, erecv, qsend, qrecv, tsend, trecv,
):
    sec = lax.axis_index("section")
    me = lax.axis_index("expert")
    core = lax.axis_index("mp")
    z = me // NY
    y = me % NY
    mine = z // 4
    other = 1 - core
    partner = (sec, me, other)

    def rcopy(src, dst, ssem, rsem, dev):
        return pltpu.make_async_remote_copy(
            src_ref=src, dst_ref=dst, send_sem=ssem, recv_sem=rsem,
            device_id=dev, device_id_type=MESH,
        )

    def wait_in(dst, rsem):
        rcopy(dst, dst, lsem.at[0], rsem, partner).wait_recv()

    def wait_out(src, ssem):
        rcopy(src, src, ssem, lsem.at[0], partner).wait_send()

    def zdev(dz):
        return (sec, ((z + dz + NZ) % NZ) * NY + y, core)

    def ydev(dy):
        return (sec, z * NY + (y + dy) % NY, core)

    def rows(start, size):
        return pl.ds(pl.multiple_of(start, size), size)

    has_next = me < NEXP - 1
    has_prev = me > 0
    active = sec > 0
    fed = sec < NSEC - 1

    barrier = pltpu.get_barrier_semaphore()

    def greet(i, carry):
        pl.semaphore_signal(
            barrier, inc=1, device_id=(sec, (me + i // 2) % NEXP, (core + i) % 2), device_id_type=MESH
        )
        return carry

    lax.fori_loop(1, 2 * NEXP, greet, 0)

    def greet_far(i, carry):
        there = ((sec + 1 + i // 8) % NSEC, z * NY + (i // 2) % NY, i % 2)
        pl.semaphore_signal(barrier, inc=1, device_id=there, device_id_type=MESH)
        return carry

    lax.fori_loop(0, 24, greet_far, 0)

    def greet_side(i, carry):
        side = me + 2 * (i % 2) - 1

        @pl.when((side >= 0) & (side < NEXP))
        def _():
            there = ((sec + 1 + i // 4) % NSEC, side, (i // 2) % 2)
            pl.semaphore_signal(barrier, inc=1, device_id=there, device_id_type=MESH)

        return carry

    lax.fori_loop(0, 12, greet_side, 0)

    halo_i_out = rcopy(ci.at[pl.ds(TOK - 16, 16)], halo_i, hsend.at[1], hrecv.at[1], (sec, me + 1, core))

    JOBS = ((2, 0, CHUNK), (1, CHUNK, HALF), (3, CHUNK + HALF, HALF))
    runs = sec >= NSEC - SPREAD

    def job_cols(job):
        return pl.ds(JOBS[job][1], JOBS[job][2])

    def ring(job, step, up_way):
        shard = (z - (step - 1) + NZ) % NZ if up_way else (z + (step - 1)) % NZ
        way = 0 if up_way else 1
        start, size = (0, TOK) if step < 4 else ((0, 64) if up_way else (64, 64))
        block = bg.at[pl.ds(pl.multiple_of(shard * TOK + start, 64), size), job_cols(job)]
        return rcopy(
            block, block, bsend.at[job, step - 1, way], brecv.at[job, step - 1, way], zdev(1 if up_way else -1)
        )

    def ring_arrived(job, step):
        for way in range(2):
            shard = (z - step + NZ) % NZ if way == 0 else (z + step) % NZ
            start, size = (0, TOK) if step < 4 else ((0, 64) if way == 0 else (64, 64))
            block = pl.ds(pl.multiple_of(shard * TOK + start, 64), size)
            wait_in(bg.at[block, job_cols(job)], brecv.at[job, step - 1, way])

    def ring_go(job, step):
        if step == 1:
            wait_in(bg.at[rows(z * TOK, TOK), job_cols(job)], jrecv.at[job, 0])
        else:
            ring_arrived(job, step - 1)
        ring(job, step, True).start()
        ring(job, step, False).start()

    def slice_of(i):
        piece = core * SPREAD + i
        return pl.ds(i * CHUNK, CHUNK), 3 - piece // 2, piece % 2

    def gifts(job, i):
        if job == 0:
            cols, to, half = slice_of(i)
        else:
            cols, to, half = pl.ds(0, HALF), 0, core
        there = job_cols(job)
        return (
            rcopy(bp.at[:, cols], bg.at[rows(z * TOK, TOK), there], jsend.at[i, 0], jrecv.at[job, 0], (to, me, half)),
            rcopy(cg.at[:, cols], gin.at[pl.ds(0, TOK), there], jsend.at[i, 1], jrecv.at[job, 1], (to, me, half)),
            rcopy(cw.at[:, cols], cwin.at[:, there], jsend.at[i, 2], jrecv.at[job, 2], (to, me, half)),
            rcopy(
                cg.at[pl.ds(0, 16), cols], gin.at[pl.ds(TOK, 16), there], jsend.at[i, 3], jrecv.at[job, 3],
                (to, me - 1, half),
            ),
        )

    def gifts_here():
        cols, there = pl.ds(CHUNK, CHUNK), job_cols(0)
        return (
            pltpu.make_async_copy(bp.at[:, cols], bg.at[rows(z * TOK, TOK), there], jrecv.at[0, 0]),
            pltpu.make_async_copy(cg.at[:, cols], gin.at[pl.ds(0, TOK), there], jrecv.at[0, 1]),
            pltpu.make_async_copy(cw.at[:, cols], cwin.at[:, there], jrecv.at[0, 2]),
        )

    def share(act, local):
        def some(copies, kinds):
            for kind in kinds:
                act(copies[kind])

        for job in (1, 2):
            @pl.when(sec == JOBS[job][0])
            def _():
                some(gifts(job, 0), (0, 1, 2))

                @pl.when(has_prev)
                def _():
                    some(gifts(job, 0), (3,))

        @pl.when(sec == 2)
        def _():
            for i in range(SPREAD):
                if i == 1:
                    @pl.when(core == 0)
                    def _():
                        some(gifts(0, 1), (0, 1, 2))

                    if local:
                        @pl.when(core == 1)
                        def _():
                            for copy in gifts_here():
                                copy.start()
                else:
                    some(gifts(0, i), (0, 1, 2))

                @pl.when(has_prev)
                def _():
                    some(gifts(0, i), (3,))

    def conv(job):
        there, width = job_cols(job), JOBS[job][2]
        wait_in(gin.at[pl.ds(0, TOK), there], jrecv.at[job, 1])
        wait_in(cwin.at[:, there], jrecv.at[job, 2])

        @pl.when(has_next)
        def _():
            wait_in(gin.at[pl.ds(TOK, 16), there], jrecv.at[job, 3])
            gext[pl.ds(TOK, 8), pl.ds(0, width)] = gin[pl.ds(TOK, 16), there].astype(F32)[0:8]

        @pl.when(jnp.logical_not(has_next))
        def _():
            gext[pl.ds(TOK, 8), pl.ds(0, width)] = jnp.zeros((8, width), F32)

        gext[pl.ds(0, TOK), pl.ds(0, width)] = gin[pl.ds(0, TOK), there].astype(F32)

        @pl.loop(0, width // 128)
        def _(i):
            lanes = pl.ds(pl.multiple_of(i * 128, 128), 128)
            cols = pl.ds(pl.multiple_of(JOBS[job][1] + i * 128, 128), 128)
            total = jnp.zeros((TOK, 128), F32)
            for tap in range(4):
                total = total + cwin[tap : tap + 1, cols] * gext[pl.ds(3 - tap, TOK), lanes]
            ag[rows(y * TOK, TOK), cols] = total.astype(BF16)

        for dy in range(1, NY):
            a_copy(job, dy).start()

    def a_copy(job, dy):
        block = ag.at[rows(y * TOK, TOK), job_cols(job)]
        return rcopy(block, block, asend.at[job, dy - 1], arecv.at[job, y], ydev(dy))

    place = NSEC - 1 - sec

    def halves(job, shard):
        return rcopy(
            psend.at[job, shard], pin.at[job, shard % 4], esend.at[job, shard % 4], erecv.at[job, shard % 4], partner
        )

    def proj_back(job, shard, dy):
        to = (y + dy) % NY
        return rcopy(
            psend.at[job, shard, rows(to * TOK, TOK)],
            prec.at[place if job == 0 else 0, y, :, rows((shard % 4) * TOK, TOK)],
            qsend.at[job, shard % 4, 0 if dy == 0 else 1], qrecv.at[place if job == 0 else 0, y],
            (JOBS[job][0] - 1, z * NY + to, core),
        )

    def proj_step(job, step):
        col, width = JOBS[job][1], JOBS[job][2]

        def one(i, carry):
            shard = (z - step + NZ) % NZ + i * ((z + step) % NZ - (z - step + NZ) % NZ)
            tall = rows(shard * TOK, TOK)
            psend[job, shard] = dot_nt(ag[:, pl.ds(col, width)], bg[tall, pl.ds(col, width)]).astype(BF16)

            @pl.when(shard // 4 != core)
            def _():
                halves(job, shard).start()

            return carry

        lax.fori_loop(0, 1 if step in (0, 4) else 2, one, 0)

    def proj_finish(job, step):
        def one(i, carry):
            shard = (z - step + NZ) % NZ + i * ((z + step) % NZ - (z - step + NZ) % NZ)

            @pl.when(shard // 4 == core)
            def _():
                wait_in(pin.at[job, shard % 4], erecv.at[job, shard % 4])
                psend[job, shard] = (psend[job, shard].astype(F32) + pin[job, shard % 4].astype(F32)).astype(BF16)
                for dy in range(1, NY):
                    proj_back(job, shard, dy).start()
                if job == 1:
                    prec[0, y, :, rows((shard % 4) * TOK, TOK)] = psend[job, shard, rows(y * TOK, TOK), :]
                else:
                    proj_back(job, shard, 0).start()

            return carry

        lax.fori_loop(0, 1 if step in (0, 4) else 2, one, 0)

    def proj_sent(job):
        def one(i, carry):
            shard = core * 4 + i
            wait_out(psend.at[job, shard, pl.ds(0, 3 * TOK)], qsend.at[job, i, 1])
            if job != 1:
                proj_back(job, shard, 0).wait_send()
            halves(job, other * 4 + i).wait_send()
            return carry

        lax.fori_loop(0, 4, one, 0)

    def tokens_arrived(job):
        for dy in range(1, NY):
            i = (y + dy) % NY
            wait_in(ag.at[rows(i * TOK, TOK), job_cols(job)], arecv.at[job, i])

    own_down = pltpu.make_async_copy(down, wdn.at[core], lsem.at[1])
    own_up = pltpu.make_async_copy(up, wup.at[core], lsem.at[2])
    own_pre = pltpu.make_async_copy(pre.at[rows(core * 256, 256)], prev_.at[core], lsem.at[3])
    give_down = rcopy(down, wdn.at[core], wsend.at[0], wrecv.at[0], partner)
    give_up = rcopy(up, wup.at[core], wsend.at[1], wrecv.at[1], partner)
    give_pre = rcopy(pre.at[rows(other * 256, 256)], prev_.at[core], wsend.at[2], wrecv.at[2], partner)
    def late(i):
        return (z + 1) % 4 + 4 * i

    def give_late(i):
        return rcopy(
            combt.at[rows(late(i) * 64, 64)], comb_late.at[pl.ds(i * 64, 64)], csend.at[i], crecv.at[i],
            (sec - 1, me, core),
        )

    def block_copy(e):
        return rcopy(
            sbuf.at[rows(e * CAP, CAP)],
            xin.at[core, rows((me % 16) * CAP, CAP)],
            xsend.at[e], xrecv.at[me % 16, core], (sec, e, mine),
        )

    def block_local(e):
        return pltpu.make_async_copy(
            sbuf.at[rows(e * CAP, CAP)],
            xin.at[core, rows((me % 16) * CAP, CAP)],
            xrecv.at[me % 16, core],
        )

    @pl.when(active)
    def _():
        own_down.start()
        own_up.start()
        own_pre.start()

        line = lax.broadcasted_iota(jnp.int32, (NEXP * CAP, TOK), 0)
        expert = line // CAP
        rank = line % CAP
        first = ids[0:1, :] == expert
        second = ids[1:2, :] == expert
        named = first | second
        gates = codes[...].astype(F32) / 256.0
        gate = jnp.where(first, gates[0:1, :], 0.0) + jnp.where(second, gates[1:2, :], 0.0)
        low = lax.broadcasted_iota(jnp.int32, (TOK, TOK), 0) < lax.broadcasted_iota(jnp.int32, (TOK, TOK), 1)
        before = jnp.dot(
            jnp.where(named, 1.0, 0.0).astype(BF16),
            jnp.where(low, 1.0, 0.0).astype(BF16),
            preferred_element_type=F32,
        )
        here = named & (before == rank.astype(F32))
        placed = jnp.where(here, gate, 0.0).astype(BF16)
        for tile in range(4):
            cols = pl.ds(tile * 512, 512)
            sbuf[:, cols] = jnp.dot(placed, og[:, cols], preferred_element_type=F32).astype(BF16)
        ones = jnp.where(here, 1.0, 0.0)
        combt[...] = ones.astype(BF16)
        comb[...] = ones.T.astype(BF16)
        for i in range(2):
            ret[rows(late(i) * 64, 64), :] = jnp.zeros((64, HALF), BF16)

    pl.semaphore_wait(barrier, 2 * NEXP - 1 + 24 + 6 * has_prev.astype(jnp.int32) + 6 * has_next.astype(jnp.int32))

    @pl.when(has_next)
    def _():
        halo_i_out.start()

    share(lambda copy: copy.start(), True)

    def dispatch(first_turn, turns):
        def send_block(i, carry):
            turn = i // 8
            zt = (z - turn + 8) % 4 + 4 * ((i // 4) % 2)
            e = zt * NY + (y + i) % NY
            own = (e == me) & (mine == core)

            @pl.when(own)
            def _():
                block_local(e).start()

            @pl.when(jnp.logical_not(own))
            def _():
                block_copy(e).start()

            return carry

        lax.fori_loop(first_turn * 8, (first_turn + turns) * 8, send_block, 0)

    both = active & runs

    @pl.when(both)
    def _():
        ring_go(0, 1)
        dispatch(0, 1)

    @pl.when(active & jnp.logical_not(runs))
    def _():
        dispatch(0, 4)

    @pl.when(active)
    def _():
        give_down.start()
        give_pre.start()
        give_up.start()
        for i in range(2):
            give_late(i).start()

    @pl.when(jnp.logical_not(active))
    def _():
        ring_go(1, 1)
        ring_go(2, 1)

    @pl.when(has_prev)
    def _():
        wait_in(halo_i, hrecv.at[1])

    @pl.when(jnp.logical_not(has_prev))
    def _():
        halo_i[...] = jnp.zeros_like(halo_i)

    iext[pl.ds(0, 8), :] = halo_i[...].astype(F32)[8:16]
    iext[pl.ds(8, TOK), :] = ci[...].astype(F32)
    tap_p[...] = jnp.zeros_like(tap_p)

    for quarter in range(4):
        @pl.loop(0, 4)
        def _(i):
            cols = pl.ds(pl.multiple_of(quarter * 512 + i * 128, 128), 128)
            lanes = pl.ds(pl.multiple_of(i * 128, 128), 128)
            grad = cg[:, cols].astype(F32)
            for tap in range(4):
                term = grad * iext[pl.ds(5 + tap, TOK), cols]
                tap_p[quarter, tap : tap + 1, lanes] = jnp.sum(term, axis=0, keepdims=True)

    def tap_scatter(dy):
        to = (y + dy) % NY
        return rcopy(tap_p.at[to], tap_r.at[y], tsend.at[0, dy - 1], trecv.at[0, y], ydev(dy))

    for dy in range(1, NY):
        tap_scatter(dy).start()

    @pl.when(runs)
    def _():
        conv(0)

    @pl.when(jnp.logical_not(active))
    def _():
        conv(1)
        conv(2)
        for job in (1, 2):
            ring_go(job, 2)

    @pl.when(both)
    def _():
        ring_go(0, 2)
        dispatch(1, 1)
        ring_go(0, 3)
        dispatch(2, 1)

    tap_r[y] = tap_p[y]
    for dy in range(1, NY):
        wait_in(tap_r.at[(y + dy) % NY], trecv.at[0, (y + dy) % NY])
    tap_s[...] = (tap_r[0] + tap_r[1]) + (tap_r[2] + tap_r[3])

    def tap_gather(dz):
        return rcopy(tap_s, tap_z.at[z], tsend.at[1, dz - 1], trecv.at[1, z], zdev(dz))

    for dz in range(1, NZ):
        tap_gather(dz).start()

    def back(src, half):
        return rcopy(
            yout.at[half, rows(src * CAP, CAP)],
            ret.at[rows(me * CAP, CAP)],
            ysend.at[src, half], yrecv.at[me],
            (sec, core * 16 + src, half),
        )

    def back_late(src, half):
        return rcopy(
            yout.at[half, rows(src * CAP, CAP)],
            ret_late.at[rows(((z // 4) * NY + y) * CAP, CAP)],
            lsend.at[src % NY, half], lrecv.at[(z // 4) * NY + y],
            (sec - 1, core * 16 + src, half),
        )

    def back_local(src):
        return pltpu.make_async_copy(
            yout.at[core, rows(src * CAP, CAP)], ret.at[rows(me * CAP, CAP)], yrecv.at[me]
        )

    def expert_chunk(turn):
        zs = (turn + z) % 4
        block = rows(zs * 64, 64)

        def arrive(i, carry):
            src = zs * NY + i // 2
            wait_in(xin.at[i % 2, rows(src * CAP, CAP)], xrecv.at[src, i % 2])
            return carry

        lax.fori_loop(0, 8, arrive, 0)
        if turn == 0:
            own_down.wait()
            wait_in(wdn.at[other], wrecv.at[0])
            own_pre.wait()
            wait_in(prev_.at[other], wrecv.at[2])
        x0 = xin[0, block, :]
        x1 = xin[1, block, :]
        grads = []
        for h in range(2):
            hidden = dot_nt(x0, wdn[h, :, 0:HALF]) + dot_nt(x1, wdn[h, :, HALF:])
            slope = silu_slope(prev_[h, block, :].astype(F32))
            grads.append((hidden * slope).astype(BF16))
        if turn == 0:
            own_up.wait()
            wait_in(wup.at[other], wrecv.at[1])
        for half in range(2):
            @pl.loop(0, 4)
            def _(t):
                wide = pl.ds(pl.multiple_of(half * HALF + t * 512, 512), 512)
                cols = pl.ds(pl.multiple_of(t * 512, 512), 512)
                value = dot_nt(grads[0], wup[0, wide, :]) + dot_nt(grads[1], wup[1, wide, :])
                yout[half, block, cols] = value.astype(BF16)

        def give(i, carry):
            src = zs * NY + (y + i // 2) % NY
            if turn == 3:
                back_late(src, i % 2).start()
                return carry
            own = (core * 16 + src == me) & (i % 2 == core)

            @pl.when(own)
            def _():
                back_local(src).start()

            @pl.when(jnp.logical_not(own))
            def _():
                back(src, i % 2).start()

            return carry

        lax.fori_loop(0, 8, give, 0)

    @pl.when(active)
    def _():
        @pl.when(runs)
        def _():
            ring_go(0, 4)
            dispatch(3, 1)

        expert_chunk(0)

        @pl.when(runs)
        def _():
            tokens_arrived(0)
            for step in range(4):
                proj_step(0, step)
            for step in range(4):
                proj_finish(0, step)

        expert_chunk(1)

        @pl.when(runs)
        def _():
            ring_arrived(0, 4)
            proj_step(0, 4)
            proj_finish(0, 4)

        expert_chunk(2)


    @pl.when(jnp.logical_not(active))
    def _():
        for job in (1, 2):
            ring_go(job, 3)
        for job in (1, 2):
            tokens_arrived(job)
            proj_step(job, 0)
            proj_step(job, 1)
            proj_finish(job, 0)
            proj_finish(job, 1)
        for job in (1, 2):
            ring_go(job, 4)
        for job in (1, 2):
            proj_step(job, 2)
            proj_step(job, 3)
            proj_finish(job, 2)
            proj_finish(job, 3)
        for job in (1, 2):
            ring_arrived(job, 4)
            proj_step(job, 4)
        for job in (1, 2):
            proj_finish(job, 4)

    tap_z[z] = tap_s[...]
    for dz in range(1, NZ):
        wait_in(tap_z.at[(z + dz) % NZ], trecv.at[1, (z + dz) % NZ])
    total = tap_z[0]
    for i in range(1, NZ):
        total = total + tap_z[i]
    tap_t[...] = total

    def tap_share(dy):
        return rcopy(tap_t, tap_o.at[y], tsend.at[2, dy - 1], trecv.at[2, y], ydev(dy))

    for dy in range(1, NY):
        tap_share(dy).start()

    def result_out(tile):
        cols = pl.ds(tile * 512, 512)
        return rcopy(res.at[:, cols], part_in.at[:, cols], osend.at[tile], orecv.at[tile], (sec - 1, me, core))

    @pl.when(active)
    def _():
        expert_chunk(3)

    @pl.when(active)
    def _():
        def arrive(i, carry):
            @pl.when((i // NY) % 4 != (z + 1) % 4)
            def _():
                wait_in(ret.at[rows(i * CAP, CAP)], yrecv.at[i])

            return carry

        lax.fori_loop(0, NEXP, arrive, 0)
        for tile in range(4):
            cols = pl.ds(tile * 512, 512)
            moe = jnp.dot(comb[...], ret[:, cols], preferred_element_type=F32)
            res[:, cols] = (og[:, cols].astype(F32) + moe).astype(BF16)
            result_out(tile).start()

    @pl.when(fed)
    def _():
        def partial(which, carry):
            for i in range(NY):
                own = (sec == 0) & (i == y)

                @pl.when(jnp.logical_not(own))
                def _():
                    wait_in(prec.at[which, i], qrecv.at[which, i])

            for i in range(NY):
                for tile in range(4):
                    cols = pl.ds((tile * NY + i) * TOK, TOK)
                    base[:, cols] += prec[which, i, :, pl.ds(tile * TOK, TOK)].astype(F32)
            return carry

        base[...] = jnp.zeros_like(base)
        lax.fori_loop(0, jnp.where(sec == 1, SPREAD, 1), partial, 0)
        for i in range(2):
            wait_in(comb_late.at[pl.ds(i * 64, 64)], crecv.at[i])
        last = comb_late[...].astype(F32).T.astype(BF16)
        for tile in range(4):
            wait_in(part_in.at[:, pl.ds(tile * 512, 512)], orecv.at[tile])

        def arrive(i, carry):
            wait_in(ret_late.at[rows(i * CAP, CAP)], lrecv.at[i])
            return carry

        lax.fori_loop(0, 8, arrive, 0)
        for tile in range(4):
            cols = pl.ds(tile * 512, 512)
            moe = jnp.dot(last, ret_late[:, cols], preferred_element_type=F32)
            out[:, cols] = (base[:, cols] + part_in[:, cols].astype(F32) + moe).astype(BF16)

    @pl.when(jnp.logical_not(fed))
    def _():
        out[...] = jnp.zeros_like(out)

    tap_o[y] = tap_t[...]
    for dy in range(1, NY):
        wait_in(tap_o.at[(y + dy) % NY], trecv.at[2, (y + dy) % NY])
    for quarter in range(4):
        kout[:, pl.ds(quarter * 512, 512)] = tap_o[quarter, 0:4, :]

    share(lambda copy: copy.wait_send(), False)

    def ring_sent(job):
        for step in range(1, 5):
            ring(job, step, True).wait_send()
            ring(job, step, False).wait_send()
        for dy in range(1, NY):
            a_copy(job, dy).wait_send()
        proj_sent(job)

    @pl.when(runs)
    def _():
        ring_sent(0)

    @pl.when(jnp.logical_not(active))
    def _():
        ring_sent(1)
        ring_sent(2)

    @pl.when(has_next)
    def _():
        halo_i_out.wait_send()

    for dy in range(1, NY):
        tap_scatter(dy).wait_send()
        tap_share(dy).wait_send()
    for dz in range(1, NZ):
        tap_gather(dz).wait_send()

    @pl.when(active)
    def _():
        give_down.wait_send()
        give_up.wait_send()
        give_pre.wait_send()
        for i in range(2):
            give_late(i).wait_send()
        for tile in range(4):
            result_out(tile).wait_send()

        def sent(e, carry):
            own = (e == me) & (mine == core)

            @pl.when(jnp.logical_not(own))
            def _():
                block_copy(e).wait_send()

            mirror = (core * 16 + e // 2 == me) & (e % 2 == core)
            final = (e // 8) % 4 == (z + 3) % 4

            @pl.when(jnp.logical_not(mirror | final))
            def _():
                back(e // 2, e % 2).wait_send()

            @pl.when(final)
            def _():
                back_late(e // 2, e % 2).wait_send()

            return carry

        lax.fori_loop(0, NEXP, sent, 0)


def shards(
    out_grad, expert_ids, gate_codes, up_weight, down_weight, pre_act, conv_grad, conv_input, conv_weight, in_proj
):
    vmem = pl.BlockSpec(memory_space=pltpu.VMEM)
    anywhere = pl.BlockSpec(memory_space=pl.ANY)
    dma = pltpu.SemaphoreType.DMA
    out, kout = pl.pallas_call(
        kernel,
        out_shape=(
            jax.ShapeDtypeStruct((TOK, HALF), BF16),
            jax.ShapeDtypeStruct((4, HALF), F32),
        ),
        in_specs=[vmem] * 7 + [anywhere] * 3,
        out_specs=(vmem, vmem),
        scratch_shapes=[
            pltpu.VMEM((2, 512, 4096), BF16),
            pltpu.VMEM((2, 4096, 512), BF16),
            pltpu.VMEM((2, 256, 512), BF16),
            pltpu.VMEM((512, HALF), BF16),
            pltpu.VMEM((2, 256, HALF), BF16),
            pltpu.VMEM((2, 256, HALF), BF16),
            pltpu.VMEM((512, HALF), BF16),
            pltpu.VMEM((TOK, 512), BF16),
            pltpu.VMEM((512, TOK), BF16),
            pltpu.VMEM((TOK, HALF), BF16),
            pltpu.VMEM((TOK, HALF), BF16),
            pltpu.VMEM((TOK, HALF), BF16),
            pltpu.VMEM((TOK, TOK), BF16),
            pltpu.VMEM((NZ * TOK, WIDE), BF16),
            pltpu.VMEM((NY * TOK, WIDE), BF16),
            pltpu.VMEM((TOK + 16, WIDE), BF16),
            pltpu.VMEM((4, WIDE), F32),
            pltpu.VMEM((16, HALF), BF16),
            pltpu.VMEM((TOK + 8, HALF), F32),
            pltpu.VMEM((TOK + 8, HALF), F32),
            pltpu.VMEM((3, NZ, NY * TOK, TOK), BF16),
            pltpu.VMEM((3, 4, NY * TOK, TOK), BF16),
            pltpu.VMEM((SPREAD, NY, TOK, 512), BF16),
            pltpu.VMEM((TOK, HALF), F32),
            pltpu.VMEM((NY, 8, 512), F32),
            pltpu.VMEM((NY, 8, 512), F32),
            pltpu.VMEM((8, 512), F32),
            pltpu.VMEM((NZ, 8, 512), F32),
            pltpu.VMEM((8, 512), F32),
            pltpu.VMEM((NY, 8, 512), F32),
            dma((5,)),
            dma((3,)), dma((3,)),
            dma((2,)), dma((2,)),
            dma((4,)), dma((4,)),
            dma((3, 4, 2)), dma((3, 4, 2)),
            dma((NEXP,)), dma((16, 2)),
            dma((16, 2)), dma((NEXP,)),
            dma((3, 3)), dma((3, NY)),
            dma((SPREAD, 4)), dma((3, 4)),
            dma((NY, 2)), dma((8,)),
            dma((2,)), dma((2,)),
            dma((3, 4)), dma((3, 4)),
            dma((3, 4, 2)), dma((SPREAD, NY)),
            dma((3, 7)), dma((3, NZ)),
        ],
        compiler_params=pltpu.CompilerParams(has_side_effects=True, collective_id=0, vmem_limit_bytes=63 * 1024 * 1024),
        name="layer_backward",
    )(
        out_grad[0], expert_ids[0].T, gate_codes[0].T, conv_grad[0], conv_input[0], conv_weight[0], in_proj[0],
        up_weight[0, 0], down_weight[0, 0], pre_act[0, 0],
    )
    return out[None], kout[None]


def solution(mesh):
    in_specs = (
        P("section", "expert", "mp"),
        P("section", "expert", None),
        P("section", "expert", None),
        P("section", "expert", None, "mp"),
        P("section", "expert", "mp", None),
        P("section", "expert", None, "mp"),
        P("section", "expert", "mp"),
        P("section", "expert", "mp"),
        P("section", None, "mp"),
        P("section", "expert", "mp"),
    )
    out_specs = (P("section", "expert", "mp"), P("section", None, "mp"))
    return jax.shard_map(shards, mesh=mesh, in_specs=in_specs, out_specs=out_specs, check_vma=False)
```

```python
import jax
import jax.numpy as jnp
from jax import lax
from jax.experimental import pallas as pl
from jax.experimental.pallas import tpu as pltpu
from jax.sharding import PartitionSpec as P

MESH = pl.DeviceIdType.MESH
F32 = jnp.float32
BF16 = jnp.bfloat16

NY = 4
NZ = 8
CAP = 16
TOK = 128
HALF = 2048
NSEC = 4
NEXP = 32
SPREAD = 2
CHUNK = 2048 // SPREAD
WIDE = CHUNK + 2 * HALF
NT = (((1,), (1,)), ((), ()))


def dot_nt(a, b):
    return lax.dot_general(a, b, NT, preferred_element_type=F32)


def silu_slope(pre_value):
    sig = 1.0 / (1.0 + jnp.exp(-pre_value))
    return sig * (1.0 + pre_value * (1.0 - sig))


def kernel(
    og, ids, codes, cg, ci, cw, bp, up, down, pre,
    out, kout,
    wdn, wup, prev_, sbuf, xin, yout, ret, comb, combt, res, part_in, ret_late, comb_late,
    bg, ag, gin, cwin, halo_i, gext, iext, psend, pin, prec, base,
    tap_p, tap_r, tap_s, tap_z, tap_t, tap_o,
    lsem, wsend, wrecv, hsend, hrecv, osend, orecv,
    bsend, brecv, xsend, xrecv, ysend, yrecv, asend, arecv,
    jsend, jrecv, lsend, lrecv, csend, crecv, esend, erecv, qsend, qrecv, tsend, trecv,
):
    sec = lax.axis_index("section")
    me = lax.axis_index("expert")
    core = lax.axis_index("mp")
    z = me // NY
    y = me % NY
    mine = z // 4
    other = 1 - core
    partner = (sec, me, other)

    def rcopy(src, dst, ssem, rsem, dev):
        return pltpu.make_async_remote_copy(
            src_ref=src, dst_ref=dst, send_sem=ssem, recv_sem=rsem,
            device_id=dev, device_id_type=MESH,
        )

    def wait_in(dst, rsem):
        rcopy(dst, dst, lsem.at[0], rsem, partner).wait_recv()

    def wait_out(src, ssem):
        rcopy(src, src, ssem, lsem.at[0], partner).wait_send()

    def zdev(dz):
        return (sec, ((z + dz + NZ) % NZ) * NY + y, core)

    def ydev(dy):
        return (sec, z * NY + (y + dy) % NY, core)

    def rows(start, size):
        return pl.ds(pl.multiple_of(start, size), size)

    has_next = me < NEXP - 1
    has_prev = me > 0
    active = sec > 0
    fed = sec < NSEC - 1

    barrier = pltpu.get_barrier_semaphore()

    def greet(i, carry):
        pl.semaphore_signal(
            barrier, inc=1, device_id=(sec, (me + i // 2) % NEXP, (core + i) % 2), device_id_type=MESH
        )
        return carry

    lax.fori_loop(1, 2 * NEXP, greet, 0)

    def greet_far(i, carry):
        there = ((sec + 1 + i // 8) % NSEC, z * NY + (i // 2) % NY, i % 2)
        pl.semaphore_signal(barrier, inc=1, device_id=there, device_id_type=MESH)
        return carry

    lax.fori_loop(0, 24, greet_far, 0)

    def greet_side(i, carry):
        side = me + 2 * (i % 2) - 1

        @pl.when((side >= 0) & (side < NEXP))
        def _():
            there = ((sec + 1 + i // 4) % NSEC, side, (i // 2) % 2)
            pl.semaphore_signal(barrier, inc=1, device_id=there, device_id_type=MESH)

        return carry

    lax.fori_loop(0, 12, greet_side, 0)

    halo_i_out = rcopy(ci.at[pl.ds(TOK - 16, 16)], halo_i, hsend.at[1], hrecv.at[1], (sec, me + 1, core))

    JOBS = ((2, 0, CHUNK), (1, CHUNK, HALF), (3, CHUNK + HALF, HALF))
    runs = sec >= NSEC - SPREAD

    def job_cols(job):
        return pl.ds(JOBS[job][1], JOBS[job][2])

    def ring(job, step, up_way):
        shard = (z - (step - 1) + NZ) % NZ if up_way else (z + (step - 1)) % NZ
        way = 0 if up_way else 1
        start, size = (0, TOK) if step < 4 else ((0, 64) if up_way else (64, 64))
        block = bg.at[pl.ds(pl.multiple_of(shard * TOK + start, 64), size), job_cols(job)]
        return rcopy(
            block, block, bsend.at[job, step - 1, way], brecv.at[job, step - 1, way], zdev(1 if up_way else -1)
        )

    def ring_arrived(job, step):
        for way in range(2):
            shard = (z - step + NZ) % NZ if way == 0 else (z + step) % NZ
            start, size = (0, TOK) if step < 4 else ((0, 64) if way == 0 else (64, 64))
            block = pl.ds(pl.multiple_of(shard * TOK + start, 64), size)
            wait_in(bg.at[block, job_cols(job)], brecv.at[job, step - 1, way])

    def ring_go(job, step):
        if step == 1:
            wait_in(bg.at[rows(z * TOK, TOK), job_cols(job)], jrecv.at[job, 0])
        else:
            ring_arrived(job, step - 1)
        ring(job, step, True).start()
        ring(job, step, False).start()

    def slice_of(i):
        piece = core * SPREAD + i
        return pl.ds(i * CHUNK, CHUNK), 3 - piece // 2, piece % 2

    def gifts(job, i):
        if job == 0:
            cols, to, half = slice_of(i)
        else:
            cols, to, half = pl.ds(0, HALF), 0, core
        there = job_cols(job)
        return (
            rcopy(bp.at[:, cols], bg.at[rows(z * TOK, TOK), there], jsend.at[i, 0], jrecv.at[job, 0], (to, me, half)),
            rcopy(cg.at[:, cols], gin.at[pl.ds(0, TOK), there], jsend.at[i, 1], jrecv.at[job, 1], (to, me, half)),
            rcopy(cw.at[:, cols], cwin.at[:, there], jsend.at[i, 2], jrecv.at[job, 2], (to, me, half)),
            rcopy(
                cg.at[pl.ds(0, 16), cols], gin.at[pl.ds(TOK, 16), there], jsend.at[i, 3], jrecv.at[job, 3],
                (to, me - 1, half),
            ),
        )

    def gifts_here():
        cols, there = pl.ds(CHUNK, CHUNK), job_cols(0)
        return (
            pltpu.make_async_copy(bp.at[:, cols], bg.at[rows(z * TOK, TOK), there], jrecv.at[0, 0]),
            pltpu.make_async_copy(cg.at[:, cols], gin.at[pl.ds(0, TOK), there], jrecv.at[0, 1]),
            pltpu.make_async_copy(cw.at[:, cols], cwin.at[:, there], jrecv.at[0, 2]),
        )

    def share(act, local):
        def some(copies, kinds):
            for kind in kinds:
                act(copies[kind])

        for job in (1, 2):
            @pl.when(sec == JOBS[job][0])
            def _():
                some(gifts(job, 0), (0, 1, 2))

                @pl.when(has_prev)
                def _():
                    some(gifts(job, 0), (3,))

        @pl.when(sec == 2)
        def _():
            for i in range(SPREAD):
                if i == 1:
                    @pl.when(core == 0)
                    def _():
                        some(gifts(0, 1), (0, 1, 2))

                    if local:
                        @pl.when(core == 1)
                        def _():
                            for copy in gifts_here():
                                copy.start()
                else:
                    some(gifts(0, i), (0, 1, 2))

                @pl.when(has_prev)
                def _():
                    some(gifts(0, i), (3,))

    def conv(job):
        there, width = job_cols(job), JOBS[job][2]
        wait_in(gin.at[pl.ds(0, TOK), there], jrecv.at[job, 1])
        wait_in(cwin.at[:, there], jrecv.at[job, 2])

        @pl.when(has_next)
        def _():
            wait_in(gin.at[pl.ds(TOK, 16), there], jrecv.at[job, 3])
            gext[pl.ds(TOK, 8), pl.ds(0, width)] = gin[pl.ds(TOK, 16), there].astype(F32)[0:8]

        @pl.when(jnp.logical_not(has_next))
        def _():
            gext[pl.ds(TOK, 8), pl.ds(0, width)] = jnp.zeros((8, width), F32)

        gext[pl.ds(0, TOK), pl.ds(0, width)] = gin[pl.ds(0, TOK), there].astype(F32)

        @pl.loop(0, width // 128)
        def _(i):
            lanes = pl.ds(pl.multiple_of(i * 128, 128), 128)
            cols = pl.ds(pl.multiple_of(JOBS[job][1] + i * 128, 128), 128)
            total = jnp.zeros((TOK, 128), F32)
            for tap in range(4):
                total = total + cwin[tap : tap + 1, cols] * gext[pl.ds(3 - tap, TOK), lanes]
            ag[rows(y * TOK, TOK), cols] = total.astype(BF16)

        for dy in range(1, NY):
            a_copy(job, dy).start()

    def a_copy(job, dy):
        block = ag.at[rows(y * TOK, TOK), job_cols(job)]
        return rcopy(block, block, asend.at[job, dy - 1], arecv.at[job, y], ydev(dy))

    place = NSEC - 1 - sec

    def halves(job, shard):
        return rcopy(
            psend.at[job, shard], pin.at[job, shard % 4], esend.at[job, shard % 4], erecv.at[job, shard % 4], partner
        )

    def proj_back(job, shard, dy):
        to = (y + dy) % NY
        return rcopy(
            psend.at[job, shard, rows(to * TOK, TOK)],
            prec.at[place if job == 0 else 0, y, :, rows((shard % 4) * TOK, TOK)],
            qsend.at[job, shard % 4, 0 if dy == 0 else 1], qrecv.at[place if job == 0 else 0, y],
            (JOBS[job][0] - 1, z * NY + to, core),
        )

    def proj_step(job, step):
        col, width = JOBS[job][1], JOBS[job][2]

        def one(i, carry):
            shard = (z - step + NZ) % NZ + i * ((z + step) % NZ - (z - step + NZ) % NZ)
            tall = rows(shard * TOK, TOK)
            psend[job, shard] = dot_nt(ag[:, pl.ds(col, width)], bg[tall, pl.ds(col, width)]).astype(BF16)

            @pl.when(shard // 4 != core)
            def _():
                halves(job, shard).start()

            return carry

        lax.fori_loop(0, 1 if step in (0, 4) else 2, one, 0)

    def proj_finish(job, step):
        def one(i, carry):
            shard = (z - step + NZ) % NZ + i * ((z + step) % NZ - (z - step + NZ) % NZ)

            @pl.when(shard // 4 == core)
            def _():
                wait_in(pin.at[job, shard % 4], erecv.at[job, shard % 4])
                psend[job, shard] = (psend[job, shard].astype(F32) + pin[job, shard % 4].astype(F32)).astype(BF16)
                for dy in range(1, NY):
                    proj_back(job, shard, dy).start()
                if job == 1:
                    prec[0, y, :, rows((shard % 4) * TOK, TOK)] = psend[job, shard, rows(y * TOK, TOK), :]
                else:
                    proj_back(job, shard, 0).start()

            return carry

        lax.fori_loop(0, 1 if step in (0, 4) else 2, one, 0)

    def proj_sent(job):
        def one(i, carry):
            shard = core * 4 + i
            wait_out(psend.at[job, shard, pl.ds(0, 3 * TOK)], qsend.at[job, i, 1])
            if job != 1:
                proj_back(job, shard, 0).wait_send()
            halves(job, other * 4 + i).wait_send()
            return carry

        lax.fori_loop(0, 4, one, 0)

    def tokens_arrived(job):
        for dy in range(1, NY):
            i = (y + dy) % NY
            wait_in(ag.at[rows(i * TOK, TOK), job_cols(job)], arecv.at[job, i])

    own_down = pltpu.make_async_copy(down, wdn.at[core], lsem.at[1])
    own_up = pltpu.make_async_copy(up, wup.at[core], lsem.at[2])
    own_pre = pltpu.make_async_copy(pre.at[rows(core * 256, 256)], prev_.at[core], lsem.at[3])
    give_down = rcopy(down, wdn.at[core], wsend.at[0], wrecv.at[0], partner)
    give_up = rcopy(up, wup.at[core], wsend.at[1], wrecv.at[1], partner)
    give_pre = rcopy(pre.at[rows(other * 256, 256)], prev_.at[core], wsend.at[2], wrecv.at[2], partner)
    def late(i):
        return (z + 1) % 4 + 4 * i

    def give_late(i):
        return rcopy(
            combt.at[rows(late(i) * 64, 64)], comb_late.at[pl.ds(i * 64, 64)], csend.at[i], crecv.at[i],
            (sec - 1, me, core),
        )

    def block_copy(e):
        return rcopy(
            sbuf.at[rows(e * CAP, CAP)],
            xin.at[core, rows((me % 16) * CAP, CAP)],
            xsend.at[e], xrecv.at[me % 16, core], (sec, e, mine),
        )

    def block_local(e):
        return pltpu.make_async_copy(
            sbuf.at[rows(e * CAP, CAP)],
            xin.at[core, rows((me % 16) * CAP, CAP)],
            xrecv.at[me % 16, core],
        )

    @pl.when(active)
    def _():
        own_down.start()
        own_up.start()
        own_pre.start()

        line = lax.broadcasted_iota(jnp.int32, (NEXP * CAP, TOK), 0)
        expert = line // CAP
        rank = line % CAP
        first = ids[0:1, :] == expert
        second = ids[1:2, :] == expert
        named = first | second
        gates = codes[...].astype(F32) / 256.0
        gate = jnp.where(first, gates[0:1, :], 0.0) + jnp.where(second, gates[1:2, :], 0.0)
        low = lax.broadcasted_iota(jnp.int32, (TOK, TOK), 0) < lax.broadcasted_iota(jnp.int32, (TOK, TOK), 1)
        before = jnp.dot(
            jnp.where(named, 1.0, 0.0).astype(BF16),
            jnp.where(low, 1.0, 0.0).astype(BF16),
            preferred_element_type=F32,
        )
        here = named & (before == rank.astype(F32))
        placed = jnp.where(here, gate, 0.0).astype(BF16)
        for tile in range(4):
            cols = pl.ds(tile * 512, 512)
            sbuf[:, cols] = jnp.dot(placed, og[:, cols], preferred_element_type=F32).astype(BF16)
        ones = jnp.where(here, 1.0, 0.0)
        combt[...] = ones.astype(BF16)
        comb[...] = ones.T.astype(BF16)
        for i in range(2):
            ret[rows(late(i) * 64, 64), :] = jnp.zeros((64, HALF), BF16)

    pl.semaphore_wait(barrier, 2 * NEXP - 1 + 24 + 6 * has_prev.astype(jnp.int32) + 6 * has_next.astype(jnp.int32))

    @pl.when(has_next)
    def _():
        halo_i_out.start()

    share(lambda copy: copy.start(), True)

    def dispatch(first_turn, turns):
        def send_block(i, carry):
            turn = i // 8
            zt = (z - turn + 8) % 4 + 4 * ((i // 4) % 2)
            e = zt * NY + (y + i) % NY
            own = (e == me) & (mine == core)

            @pl.when(own)
            def _():
                block_local(e).start()

            @pl.when(jnp.logical_not(own))
            def _():
                block_copy(e).start()

            return carry

        lax.fori_loop(first_turn * 8, (first_turn + turns) * 8, send_block, 0)

    both = active & runs

    @pl.when(both)
    def _():
        ring_go(0, 1)
        dispatch(0, 1)

    @pl.when(active & jnp.logical_not(runs))
    def _():
        dispatch(0, 4)

    @pl.when(active)
    def _():
        give_down.start()
        give_pre.start()
        give_up.start()
        for i in range(2):
            give_late(i).start()

    @pl.when(jnp.logical_not(active))
    def _():
        ring_go(1, 1)
        ring_go(2, 1)

    @pl.when(has_prev)
    def _():
        wait_in(halo_i, hrecv.at[1])

    @pl.when(jnp.logical_not(has_prev))
    def _():
        halo_i[...] = jnp.zeros_like(halo_i)

    iext[pl.ds(0, 8), :] = halo_i[...].astype(F32)[8:16]
    iext[pl.ds(8, TOK), :] = ci[...].astype(F32)
    tap_p[...] = jnp.zeros_like(tap_p)

    for quarter in range(4):
        @pl.loop(0, 4)
        def _(i):
            cols = pl.ds(pl.multiple_of(quarter * 512 + i * 128, 128), 128)
            lanes = pl.ds(pl.multiple_of(i * 128, 128), 128)
            grad = cg[:, cols].astype(F32)
            for tap in range(4):
                term = grad * iext[pl.ds(5 + tap, TOK), cols]
                tap_p[quarter, tap : tap + 1, lanes] = jnp.sum(term, axis=0, keepdims=True)

    def tap_scatter(dy):
        to = (y + dy) % NY
        return rcopy(tap_p.at[to], tap_r.at[y], tsend.at[0, dy - 1], trecv.at[0, y], ydev(dy))

    for dy in range(1, NY):
        tap_scatter(dy).start()

    @pl.when(runs)
    def _():
        conv(0)

    @pl.when(jnp.logical_not(active))
    def _():
        conv(1)
        conv(2)
        for job in (1, 2):
            ring_go(job, 2)

    @pl.when(both)
    def _():
        ring_go(0, 2)
        dispatch(1, 1)
        ring_go(0, 3)
        dispatch(2, 1)

    tap_r[y] = tap_p[y]
    for dy in range(1, NY):
        wait_in(tap_r.at[(y + dy) % NY], trecv.at[0, (y + dy) % NY])
    tap_s[...] = (tap_r[0] + tap_r[1]) + (tap_r[2] + tap_r[3])

    def tap_gather(dz):
        return rcopy(tap_s, tap_z.at[z], tsend.at[1, dz - 1], trecv.at[1, z], zdev(dz))

    for dz in range(1, NZ):
        tap_gather(dz).start()

    def back(src, half):
        return rcopy(
            yout.at[half, rows(src * CAP, CAP)],
            ret.at[rows(me * CAP, CAP)],
            ysend.at[src, half], yrecv.at[me],
            (sec, core * 16 + src, half),
        )

    def back_late(src, half):
        return rcopy(
            yout.at[half, rows(src * CAP, CAP)],
            ret_late.at[rows(((z // 4) * NY + y) * CAP, CAP)],
            lsend.at[src % NY, half], lrecv.at[(z // 4) * NY + y],
            (sec - 1, core * 16 + src, half),
        )

    def back_local(src):
        return pltpu.make_async_copy(
            yout.at[core, rows(src * CAP, CAP)], ret.at[rows(me * CAP, CAP)], yrecv.at[me]
        )

    def expert_chunk(turn):
        zs = (turn + z) % 4
        block = rows(zs * 64, 64)

        def arrive(i, carry):
            src = zs * NY + i // 2
            wait_in(xin.at[i % 2, rows(src * CAP, CAP)], xrecv.at[src, i % 2])
            return carry

        lax.fori_loop(0, 8, arrive, 0)
        if turn == 0:
            own_down.wait()
            wait_in(wdn.at[other], wrecv.at[0])
            own_pre.wait()
            wait_in(prev_.at[other], wrecv.at[2])
        x0 = xin[0, block, :]
        x1 = xin[1, block, :]
        grads = []
        for h in range(2):
            hidden = dot_nt(x0, wdn[h, :, 0:HALF]) + dot_nt(x1, wdn[h, :, HALF:])
            slope = silu_slope(prev_[h, block, :].astype(F32))
            grads.append((hidden * slope).astype(BF16))
        if turn == 0:
            own_up.wait()
            wait_in(wup.at[other], wrecv.at[1])
        for half in range(2):
            @pl.loop(0, 4)
            def _(t):
                wide = pl.ds(pl.multiple_of(half * HALF + t * 512, 512), 512)
                cols = pl.ds(pl.multiple_of(t * 512, 512), 512)
                value = dot_nt(grads[0], wup[0, wide, :]) + dot_nt(grads[1], wup[1, wide, :])
                yout[half, block, cols] = value.astype(BF16)

        def give(i, carry):
            src = zs * NY + (y + i // 2) % NY
            if turn == 3:
                back_late(src, i % 2).start()
                return carry
            own = (core * 16 + src == me) & (i % 2 == core)

            @pl.when(own)
            def _():
                back_local(src).start()

            @pl.when(jnp.logical_not(own))
            def _():
                back(src, i % 2).start()

            return carry

        lax.fori_loop(0, 8, give, 0)

    @pl.when(active)
    def _():
        @pl.when(runs)
        def _():
            ring_go(0, 4)
            dispatch(3, 1)

        expert_chunk(0)

        @pl.when(runs)
        def _():
            tokens_arrived(0)
            for step in range(4):
                proj_step(0, step)
            for step in range(4):
                proj_finish(0, step)

        expert_chunk(1)

        @pl.when(runs)
        def _():
            ring_arrived(0, 4)
            proj_step(0, 4)
            proj_finish(0, 4)

        expert_chunk(2)


    @pl.when(jnp.logical_not(active))
    def _():
        for job in (1, 2):
            ring_go(job, 3)
        for job in (1, 2):
            tokens_arrived(job)
            proj_step(job, 0)
            proj_step(job, 1)
        for job in (1, 2):
            ring_go(job, 4)
        for job in (1, 2):
            proj_finish(job, 0)
            proj_finish(job, 1)
            proj_step(job, 2)
            proj_step(job, 3)
            proj_finish(job, 2)
            proj_finish(job, 3)
        for job in (1, 2):
            ring_arrived(job, 4)
            proj_step(job, 4)
        for job in (1, 2):
            proj_finish(job, 4)

    tap_z[z] = tap_s[...]
    for dz in range(1, NZ):
        wait_in(tap_z.at[(z + dz) % NZ], trecv.at[1, (z + dz) % NZ])
    total = tap_z[0]
    for i in range(1, NZ):
        total = total + tap_z[i]
    tap_t[...] = total

    def tap_share(dy):
        return rcopy(tap_t, tap_o.at[y], tsend.at[2, dy - 1], trecv.at[2, y], ydev(dy))

    for dy in range(1, NY):
        tap_share(dy).start()

    def result_out(tile):
        cols = pl.ds(tile * 512, 512)
        return rcopy(res.at[:, cols], part_in.at[:, cols], osend.at[tile], orecv.at[tile], (sec - 1, me, core))

    @pl.when(active)
    def _():
        expert_chunk(3)

    @pl.when(active)
    def _():
        def arrive(i, carry):
            @pl.when((i // NY) % 4 != (z + 1) % 4)
            def _():
                wait_in(ret.at[rows(i * CAP, CAP)], yrecv.at[i])

            return carry

        lax.fori_loop(0, NEXP, arrive, 0)
        for tile in range(4):
            cols = pl.ds(tile * 512, 512)
            moe = jnp.dot(comb[...], ret[:, cols], preferred_element_type=F32)
            res[:, cols] = (og[:, cols].astype(F32) + moe).astype(BF16)
            result_out(tile).start()

    @pl.when(fed)
    def _():
        def partial(which, carry):
            for i in range(NY):
                own = (sec == 0) & (i == y)

                @pl.when(jnp.logical_not(own))
                def _():
                    wait_in(prec.at[which, i], qrecv.at[which, i])

            for i in range(NY):
                for tile in range(4):
                    cols = pl.ds((tile * NY + i) * TOK, TOK)
                    base[:, cols] += prec[which, i, :, pl.ds(tile * TOK, TOK)].astype(F32)
            return carry

        base[...] = jnp.zeros_like(base)
        lax.fori_loop(0, jnp.where(sec == 1, SPREAD, 1), partial, 0)
        for i in range(2):
            wait_in(comb_late.at[pl.ds(i * 64, 64)], crecv.at[i])
        last = comb_late[...].astype(F32).T.astype(BF16)
        for tile in range(4):
            wait_in(part_in.at[:, pl.ds(tile * 512, 512)], orecv.at[tile])

        def arrive(i, carry):
            wait_in(ret_late.at[rows(i * CAP, CAP)], lrecv.at[i])
            return carry

        lax.fori_loop(0, 8, arrive, 0)
        for tile in range(4):
            cols = pl.ds(tile * 512, 512)
            moe = jnp.dot(last, ret_late[:, cols], preferred_element_type=F32)
            out[:, cols] = (base[:, cols] + part_in[:, cols].astype(F32) + moe).astype(BF16)

    @pl.when(jnp.logical_not(fed))
    def _():
        out[...] = jnp.zeros_like(out)

    tap_o[y] = tap_t[...]
    for dy in range(1, NY):
        wait_in(tap_o.at[(y + dy) % NY], trecv.at[2, (y + dy) % NY])
    for quarter in range(4):
        kout[:, pl.ds(quarter * 512, 512)] = tap_o[quarter, 0:4, :]

    share(lambda copy: copy.wait_send(), False)

    def ring_sent(job):
        for step in range(1, 5):
            ring(job, step, True).wait_send()
            ring(job, step, False).wait_send()
        for dy in range(1, NY):
            a_copy(job, dy).wait_send()
        proj_sent(job)

    @pl.when(runs)
    def _():
        ring_sent(0)

    @pl.when(jnp.logical_not(active))
    def _():
        ring_sent(1)
        ring_sent(2)

    @pl.when(has_next)
    def _():
        halo_i_out.wait_send()

    for dy in range(1, NY):
        tap_scatter(dy).wait_send()
        tap_share(dy).wait_send()
    for dz in range(1, NZ):
        tap_gather(dz).wait_send()

    @pl.when(active)
    def _():
        give_down.wait_send()
        give_up.wait_send()
        give_pre.wait_send()
        for i in range(2):
            give_late(i).wait_send()
        for tile in range(4):
            result_out(tile).wait_send()

        def sent(e, carry):
            own = (e == me) & (mine == core)

            @pl.when(jnp.logical_not(own))
            def _():
                block_copy(e).wait_send()

            mirror = (core * 16 + e // 2 == me) & (e % 2 == core)
            final = (e // 8) % 4 == (z + 3) % 4

            @pl.when(jnp.logical_not(mirror | final))
            def _():
                back(e // 2, e % 2).wait_send()

            @pl.when(final)
            def _():
                back_late(e // 2, e % 2).wait_send()

            return carry

        lax.fori_loop(0, NEXP, sent, 0)


def shards(
    out_grad, expert_ids, gate_codes, up_weight, down_weight, pre_act, conv_grad, conv_input, conv_weight, in_proj
):
    vmem = pl.BlockSpec(memory_space=pltpu.VMEM)
    anywhere = pl.BlockSpec(memory_space=pl.ANY)
    dma = pltpu.SemaphoreType.DMA
    out, kout = pl.pallas_call(
        kernel,
        out_shape=(
            jax.ShapeDtypeStruct((TOK, HALF), BF16),
            jax.ShapeDtypeStruct((4, HALF), F32),
        ),
        in_specs=[vmem] * 7 + [anywhere] * 3,
        out_specs=(vmem, vmem),
        scratch_shapes=[
            pltpu.VMEM((2, 512, 4096), BF16),
            pltpu.VMEM((2, 4096, 512), BF16),
            pltpu.VMEM((2, 256, 512), BF16),
            pltpu.VMEM((512, HALF), BF16),
            pltpu.VMEM((2, 256, HALF), BF16),
            pltpu.VMEM((2, 256, HALF), BF16),
            pltpu.VMEM((512, HALF), BF16),
            pltpu.VMEM((TOK, 512), BF16),
            pltpu.VMEM((512, TOK), BF16),
            pltpu.VMEM((TOK, HALF), BF16),
            pltpu.VMEM((TOK, HALF), BF16),
            pltpu.VMEM((TOK, HALF), BF16),
            pltpu.VMEM((TOK, TOK), BF16),
            pltpu.VMEM((NZ * TOK, WIDE), BF16),
            pltpu.VMEM((NY * TOK, WIDE), BF16),
            pltpu.VMEM((TOK + 16, WIDE), BF16),
            pltpu.VMEM((4, WIDE), F32),
            pltpu.VMEM((16, HALF), BF16),
            pltpu.VMEM((TOK + 8, HALF), F32),
            pltpu.VMEM((TOK + 8, HALF), F32),
            pltpu.VMEM((3, NZ, NY * TOK, TOK), BF16),
            pltpu.VMEM((3, 4, NY * TOK, TOK), BF16),
            pltpu.VMEM((SPREAD, NY, TOK, 512), BF16),
            pltpu.VMEM((TOK, HALF), F32),
            pltpu.VMEM((NY, 8, 512), F32),
            pltpu.VMEM((NY, 8, 512), F32),
            pltpu.VMEM((8, 512), F32),
            pltpu.VMEM((NZ, 8, 512), F32),
            pltpu.VMEM((8, 512), F32),
            pltpu.VMEM((NY, 8, 512), F32),
            dma((5,)),
            dma((3,)), dma((3,)),
            dma((2,)), dma((2,)),
            dma((4,)), dma((4,)),
            dma((3, 4, 2)), dma((3, 4, 2)),
            dma((NEXP,)), dma((16, 2)),
            dma((16, 2)), dma((NEXP,)),
            dma((3, 3)), dma((3, NY)),
            dma((SPREAD, 4)), dma((3, 4)),
            dma((NY, 2)), dma((8,)),
            dma((2,)), dma((2,)),
            dma((3, 4)), dma((3, 4)),
            dma((3, 4, 2)), dma((SPREAD, NY)),
            dma((3, 7)), dma((3, NZ)),
        ],
        compiler_params=pltpu.CompilerParams(has_side_effects=True, collective_id=0, vmem_limit_bytes=63 * 1024 * 1024),
        name="layer_backward",
    )(
        out_grad[0], expert_ids[0].T, gate_codes[0].T, conv_grad[0], conv_input[0], conv_weight[0], in_proj[0],
        up_weight[0, 0], down_weight[0, 0], pre_act[0, 0],
    )
    return out[None], kout[None]


def solution(mesh):
    in_specs = (
        P("section", "expert", "mp"),
        P("section", "expert", None),
        P("section", "expert", None),
        P("section", "expert", None, "mp"),
        P("section", "expert", "mp", None),
        P("section", "expert", None, "mp"),
        P("section", "expert", "mp"),
        P("section", "expert", "mp"),
        P("section", None, "mp"),
        P("section", "expert", "mp"),
    )
    out_specs = (P("section", "expert", "mp"), P("section", None, "mp"))
    return jax.shard_map(shards, mesh=mesh, in_specs=in_specs, out_specs=out_specs, check_vma=False)
```
